512 devices in a mesh: track: 64 (over y, z), cam: 8 (over x, core).
Axes of the slice: x: 4, y: 8, z: 8, core: 2. Of those that a mesh axis runs over, the one named last changes fastest.
Arguments:
- omega: bfloat16 [32, 9, 65536], P(None, None, ('track', 'cam')), may hold values from -6 to 6
- u_blocks: float32 [9, 9, 65536], P(None, None, ('track', 'cam')), may hold values from -5.4 to 36, as said below
- w_blocks: bfloat16 [9, 3, 262144], P(None, None, ('track', 'cam')), may hold values from -1.796875 to 1.796875
- v_inverse: float32 [3, 3, 65536], P(None, None, ('track', 'cam')), may hold values from -0.6 to 1.5, as said below
- obs_camera: int32 [262144], P(('track', 'cam')), may hold values from 0 to 65535, as said below
- obs_track: int32 [262144], P(('track', 'cam')), may hold values from 0 to 31, as said below
- obs_mask: int32 [262144], P(('track', 'cam')), may hold values from 0 to 1, as said below
Outputs:
- sketch: float32 [32, 9, 65536], P(None, None, ('track', 'cam'))
- basis: float32 [32, 9, 65536], P(None, None, ('track', 'cam'))
- factor: float32 [32, 32], replicated
The draws below stay inside these ranges and needn't reach their ends.
Inputs may be any that keep to these rules, and one draw needn't show every extreme that they name: `obs_camera`: cameras c * 128 to (c + 1) * 128 - 1 belong to device c (track slower). Among one device's 512 observations, padding included, at most 2 name cameras of any one device, and exactly 2 name those of some device. `obs_track`: in each aligned block of 128 observations, slots 0 to 31 each hold one track of 2 to 4 consecutive observations from the block's start, in rising order; the padding after them carries slot 31. `obs_mask`: 1 on the observations of tracks, 0 on the padding at the end of each block. `u_blocks`: each block is symmetric. `v_inverse`: each block is symmetric positive definite.
All inputs are finite; a program needn't handle non-finite values.
Results may differ from the reference program's by a relative error of at most 0.00095.
Values may be sent and summed in bfloat16 or wider, within the bound.
No kernel may reach another device: no remote copies, remote signals or barrier semaphores. Data moves between devices by JAX's collectives and lax.ppermute only.
A program may use at most 64 MiB of HBM per device.

```python
import math
import jax
import jax.numpy as jnp
from jax import lax

CAM_PARAMS = 9
COLS = 32
BLK_OBS = 128
TRK_BLK = 32
CAM_DEV = 128
OBS_DEV = 512
CAMS = 65536
OBS = 262144
TRACKS = 65536


def track_layout(key):
    blocks = OBS // BLK_OBS
    lengths = jax.random.randint(key, (blocks, TRK_BLK), 2, 5)
    ends = jnp.cumsum(lengths, axis=1)
    position = jnp.arange(BLK_OBS, dtype=jnp.int32)
    slot_ids = jnp.sum((position[None, :, None] >= ends[:, None, :]).astype(jnp.int32), axis=2)
    live_ids = (slot_ids < TRK_BLK).astype(jnp.int32)
    slot_ids = jnp.minimum(slot_ids, TRK_BLK - 1)
    return (slot_ids.reshape(-1).astype(jnp.int32), live_ids.reshape(-1))


def draw_obs_track(key, part):
    return track_layout(jax.random.fold_in(key, 11))[0]


def draw_obs_mask(key, part):
    return track_layout(jax.random.fold_in(key, 11))[1]


def draw_obs_camera(key, part):
    device_count = OBS // OBS_DEV
    capacity = max(2, 2 * OBS_DEV // device_count)
    slot_total = device_count * capacity

    def one_device(device_key):
        keys = jax.random.split(device_key, 5)
        heat = jax.random.randint(keys[0], (device_count,), 0, 4)
        full_owner = jax.random.randint(keys[1], (), 0, device_count)
        owner_of = jnp.arange(slot_total, dtype=jnp.int32) // capacity
        score = jax.random.randint(keys[2], (slot_total,), 0, 65536) + heat[owner_of] * 16384
        score = jnp.where(owner_of == full_owner, score + 1048576, score)
        picked = jnp.argsort(-score, stable=True)[:OBS_DEV]
        cameras = owner_of[picked] * CAM_DEV + jax.random.randint(keys[3], (OBS_DEV,), 0, CAM_DEV)
        return cameras[jax.random.permutation(keys[4], OBS_DEV)]
    return jax.vmap(one_device)(jax.random.split(key, device_count)).reshape(-1).astype(jnp.int32)


def draw_u_blocks(key, part):
    keys = jax.random.split(key, 2)
    cam_index = jnp.arange(CAMS, dtype=jnp.float32)
    growth = 2.0
    scaling = 1.0 + growth * cam_index / (CAMS - 1)
    diagonal = jax.random.uniform(keys[0], (9, CAMS), jnp.float32, 2.0, 4.0)
    rough = jax.random.uniform(keys[1], (9, 9, CAMS), jnp.float32, -0.6, 0.6)
    symmetric = 0.5 * (rough + rough.transpose(1, 0, 2))
    identity = jnp.eye(9, dtype=jnp.float32)[:, :, None]
    blocks = symmetric * (1.0 - identity) + identity * diagonal[:, None, :]
    return (blocks * scaling[None, None, :]).astype(jnp.float32)


def draw_v_inverse(key, part):
    keys = jax.random.split(key, 2)
    low_end, high_end = (0.3, 1.0)
    diagonal = jnp.exp(jax.random.uniform(keys[0], (3, TRACKS), jnp.float32, math.log(low_end), math.log(high_end)))
    rough = jax.random.uniform(keys[1], (3, 3, TRACKS), jnp.float32, -1.0, 1.0)
    symmetric = 0.5 * (rough + rough.transpose(1, 0, 2))
    root_diag = jnp.sqrt(diagonal)
    coupling = 0.4 * symmetric * root_diag[:, None, :] * root_diag[None, :, :]
    identity = jnp.eye(3, dtype=jnp.float32)[:, :, None]
    return (coupling * (1.0 - identity) + identity * diagonal[:, None, :]).astype(jnp.float32)


def shard_levels(rng, shape, pieces, smallest, high):
    def one(axis_at, blocks):
        draws = jax.random.uniform(jax.random.fold_in(jax.random.fold_in(rng, 6), axis_at), (blocks,), jnp.float32, smallest / len(pieces), high / len(pieces))
        return jnp.repeat(jnp.exp(draws), shape[axis_at] // blocks).reshape((-1,) + (1,) * (len(shape) - axis_at - 1))

    loudness = one(*pieces[0])
    for cut in pieces[1:]:
        loudness = loudness * one(*cut)
    return loudness


def noise(rng, dims, width, most, shards=(), held_as=jnp.bfloat16):
    entries = jax.random.normal(rng, dims, jnp.float32) * width
    if len(shards) > 0:
        entries = shard_levels(rng, dims, shards, -0.22, 0.18) * entries
    return jnp.clip(entries, min=-most, max=most).astype(held_as)


def setup_inputs(seed: int = 0) -> dict:
    key_list = jax.random.split(jax.random.key(seed), 8)
    omega = noise(key_list[0], (COLS, CAM_PARAMS, CAMS), 1.0, 6.0, ((2, 512),))
    u_blocks = draw_u_blocks(jax.random.fold_in(key_list[7], 71), 0)
    w_blocks = noise(key_list[2], (CAM_PARAMS, 3, OBS), 0.3, 1.796875, ((2, 512),))
    v_inverse = draw_v_inverse(jax.random.fold_in(key_list[7], 71), 0)
    obs_camera = draw_obs_camera(jax.random.fold_in(key_list[7], 71), 0)
    obs_track = draw_obs_track(jax.random.fold_in(key_list[7], 71), 0)
    obs_mask = draw_obs_mask(jax.random.fold_in(key_list[7], 71), 0)
    return {"omega": omega, "u_blocks": u_blocks, "w_blocks": w_blocks, "v_inverse": v_inverse, "obs_camera": obs_camera, "obs_track": obs_track, "obs_mask": obs_mask}


HIGH = lax.Precision.HIGHEST

def eliminate(gathered, weight, inverse, slot_ids, live_ids):
    live_mask = live_ids.astype(jnp.float32)
    track_ids = jnp.arange(OBS_DEV, dtype=jnp.int32) // BLK_OBS * TRK_BLK + slot_ids
    weight_f = weight.astype(jnp.float32)
    projected = jnp.einsum('mio,mco->ico', weight_f, gathered.astype(jnp.float32), precision=HIGH) * live_mask
    track_sum = jax.ops.segment_sum(projected.transpose(2, 0, 1), track_ids, num_segments=OBS_DEV // BLK_OBS * TRK_BLK)
    solved = jnp.einsum('ijt,tjc->tic', inverse, track_sum, precision=HIGH)
    spread = solved[track_ids]
    returned = jnp.einsum('mio,oic->mco', weight_f, spread, precision=HIGH) * live_mask
    return returned.astype(jnp.bfloat16)

def reference(omega, u_blocks, w_blocks, v_inverse, obs_camera, obs_track, obs_mask):
    device_count = OBS // OBS_DEV
    tracks_dev = OBS_DEV // BLK_OBS * TRK_BLK
    weights = w_blocks.reshape(9, 3, device_count, OBS_DEV).transpose(2, 0, 1, 3)
    inverses = v_inverse.reshape(3, 3, device_count, tracks_dev).transpose(2, 0, 1, 3)
    cameras = obs_camera.reshape(device_count, OBS_DEV)
    slots = obs_track.reshape(device_count, OBS_DEV)
    masks = obs_mask.reshape(device_count, OBS_DEV)

    def visit_device(accumulated, device_part):
        weight, inverse, camera, slot_ids, live_ids = device_part
        gathered = jnp.take(omega, camera, axis=2).transpose(1, 0, 2)
        returned = eliminate(gathered, weight, inverse, slot_ids, live_ids)
        accumulated = accumulated.at[:, :, camera].add(returned.astype(jnp.float32).transpose(1, 0, 2))
        return (accumulated, None)
    accumulated, _ = lax.scan(visit_device, jnp.zeros(omega.shape, jnp.float32), (weights, inverses, cameras, slots, masks))
    own_term = jnp.einsum('mnk,jnk->jmk', u_blocks.astype(jnp.float32), omega.astype(jnp.float32), precision=HIGH)
    sketch = own_term - accumulated
    flat_rows = sketch.reshape(sketch.shape[0], -1)
    gram_matrix = jnp.dot(flat_rows.astype(jnp.float32), flat_rows.T.astype(jnp.float32), precision=HIGH, preferred_element_type=jnp.float32)
    lower_factor = jnp.linalg.cholesky(gram_matrix / flat_rows.shape[1])
    basis_rows = jax.scipy.linalg.solve_triangular(lower_factor, flat_rows, lower=True).reshape(sketch.shape)
    return (sketch, basis_rows, lower_factor.T)
```

```python
import functools

import jax
import jax.numpy as jnp
from jax import lax
from jax.experimental import pallas as pl
from jax.experimental.pallas import tpu as pltpu
from jax.sharding import Mesh
from jax.sharding import PartitionSpec as P

BLK_OBS = 128
TRK_BLK = 32
LANES = 128
PARAMS = 9
COLS = 32
TRACK = ("track_0", "track_1")
CAM = ("cam_0", "cam_1")
TRACK_CAM = TRACK + CAM
HIGH = lax.Precision.HIGHEST
F32 = jnp.float32
BF16 = jnp.bfloat16


def dot_lanes(lhs, rhs):
    return lax.dot_general(lhs, rhs, (((1,), (1,)), ((), ())), preferred_element_type=F32)


def call(kernel, shapes, *args, scratch=()):
    return pl.pallas_call(
        kernel,
        out_shape=tuple(jax.ShapeDtypeStruct(s, d) for s, d in shapes),
        scratch_shapes=list(scratch),
        compiler_params=pltpu.CompilerParams(vmem_limit_bytes=48 << 20),
    )(*args)


def request_kernel(capacity, camera_ref, mask_ref, w_ref, request_ref, slot_ref, rows):
    obs = camera_ref.shape[1]
    camera = camera_ref[...]
    owner = lax.shift_right_logical(camera, 7)
    owner_f = owner.astype(F32)
    blocks = obs // LANES
    sub = lax.broadcasted_iota(jnp.int32, (LANES, LANES), 0)
    lane = lax.broadcasted_iota(jnp.int32, (LANES, LANES), 1)
    row_of = [owner_f[:, LANES * b : LANES * (b + 1)] for b in range(blocks)]
    column_of = [jnp.broadcast_to(r, (LANES, LANES)).T for r in row_of]
    ranks = []
    for q in range(blocks):
        same = jnp.where((column_of[q] == row_of[q]) & (sub < lane), 1.0, 0.0)
        for b in range(q):
            same = same + jnp.where(column_of[b] == row_of[q], 1.0, 0.0)
        ranks.append(jnp.sum(same, axis=0, keepdims=True))
    slot = owner * capacity + jnp.concatenate(ranks, axis=1).astype(jnp.int32)
    slot_ref[...] = slot
    live = mask_ref[...].astype(F32)
    rows[...] = jnp.zeros(rows.shape, F32)
    for m in range(PARAMS):
        rows[3 * m : 3 * m + 3, :] = w_ref[m].astype(F32) * live
    rows[3 * PARAMS : 3 * PARAMS + 1, :] = (camera & (LANES - 1)).astype(F32)
    values = rows[...].astype(BF16)
    slots = request_ref.shape[0]
    step = 256
    for s in range(0, slots, step):
        ids = lax.broadcasted_iota(jnp.int32, (step, obs), 0) + s
        chosen = jnp.where(ids == slot, 1.0, 0.0).astype(BF16)
        request_ref[s : s + step, :] = dot_lanes(chosen, values).astype(BF16)


def member_kernel(slot_ref, track_ref, by_track_ref, by_slot_ref):
    obs = slot_ref.shape[1]
    tracks, slots = by_track_ref.shape
    position = lax.broadcasted_iota(jnp.int32, (1, obs), 1)
    track = lax.shift_right_logical(position, 7) * TRK_BLK + track_ref[...]
    ids = lax.broadcasted_iota(jnp.int32, (tracks, obs), 0)
    member = jnp.where(ids == track, 1.0, 0.0).astype(BF16)
    step = 256
    for s in range(0, slots, step):
        ids = lax.broadcasted_iota(jnp.int32, (step, obs), 0) + s
        chosen = jnp.where(ids == slot_ref[...], 1.0, 0.0).astype(BF16)
        by_track_ref[:, s : s + step] = dot_lanes(member, chosen).astype(BF16)
        by_slot_ref[s : s + step, :] = dot_lanes(chosen, member).astype(BF16)


def spread_of(width):
    row = lax.broadcasted_iota(jnp.int32, (LANES, width), 0)
    lane = lax.broadcasted_iota(jnp.int32, (LANES, width), 1)
    third = lax.shift_right_logical(lane & (LANES - 1), 5)
    wanted = 3 * lax.shift_right_logical(lane, 7) + third
    return jnp.where((row == wanted) & (third < 3), 1.0, 0.0).astype(BF16)


def row_everywhere(index):
    row = lax.broadcasted_iota(jnp.int32, (LANES, LANES), 0)
    return jnp.where(row == index, 1.0, 0.0).astype(BF16)


def dot(lhs, rhs):
    return jnp.dot(lhs, rhs, preferred_element_type=F32)


def camera_onehot(request):
    local = dot(request, row_everywhere(3 * PARAMS))
    lane = lax.broadcasted_iota(jnp.int32, local.shape, 1).astype(F32)
    return local == lane


def project_kernel(request_ref, table_ref, reply_ref):
    spread = spread_of(PARAMS * LANES)
    step = 256
    for s in range(0, request_ref.shape[0], step):
        request = request_ref[s : s + step, :]
        chosen = jnp.where(camera_onehot(request), 1.0, 0.0).astype(BF16)
        total = jnp.zeros((step, LANES), F32)
        for m in range(PARAMS):
            block = slice(LANES * m, LANES * (m + 1))
            total = total + dot_lanes(chosen, table_ref[block, :]) * dot(request, spread[:, block])
        reply_ref[s : s + step, :] = total.astype(BF16)


def solve_kernel(reply_ref, by_track_ref, by_slot_ref, v_ref, out_ref):
    summed = dot(by_track_ref[...], reply_ref[...]).T
    parts = []
    for i in range(3):
        part = jnp.zeros((COLS, LANES), F32)
        for k in range(3):
            part = part + v_ref[i, k : k + 1, :] * summed[COLS * k : COLS * (k + 1), :]
        parts.append(part)
    parts.append(jnp.zeros((LANES - 3 * COLS, LANES), F32))
    solved = jnp.concatenate(parts, axis=0).astype(BF16)
    out_ref[...] = dot_lanes(by_slot_ref[...], solved).astype(BF16)


def weights_kernel(request_ref, omega_ref, u_ref, weights_ref, own_ref):
    slots = request_ref.shape[0]
    step = 256
    for s in range(0, slots, step):
        request = request_ref[s : s + step, :]
        chosen = camera_onehot(request)
        for i in range(3):
            for m in range(PARAMS):
                spread = dot(request, row_everywhere(3 * m + i))
                weights_ref[i * slots + s : i * slots + s + step, LANES * m : LANES * (m + 1)] = (
                    jnp.where(chosen, spread, 0.0).astype(BF16)
                )
    table = [omega_ref[n].astype(F32) for n in range(PARAMS)]
    for m in range(PARAMS):
        total = jnp.zeros((COLS, LANES), F32)
        for n in range(PARAMS):
            total = total + u_ref[m, n : n + 1, :] * table[n]
        own_ref[:, LANES * m : LANES * (m + 1)] = total


def sketch_kernel(solved_ref, weights_ref, own_ref, sketch_ref, gram_ref):
    slots = solved_ref.shape[0]
    turned = solved_ref[...].astype(F32).T.astype(BF16)
    sketch = own_ref[...]
    for i in range(3):
        sketch = sketch - dot(
            turned[COLS * i : COLS * (i + 1), :], weights_ref[i * slots : (i + 1) * slots, :]
        )
    sketch_ref[...] = sketch
    gram = lax.dot_general(
        sketch, sketch, (((1,), (1,)), ((), ())), precision=HIGH, preferred_element_type=F32
    )
    packed = jnp.concatenate([gram[8 * q : 8 * q + 8, :] for q in range(4)], axis=1)
    gram_ref[...] = jnp.broadcast_to(packed[None], gram_ref.shape)


def gather_kernel(parts_ref, out_ref):
    out_ref[...] = jnp.broadcast_to(jnp.sum(parts_ref[...], axis=0)[None], out_ref.shape)


def finish_kernel(row_total, parts_ref, sketch_ref, basis_ref, factor_ref):
    packed = jnp.sum(parts_ref[...], axis=0) / row_total
    gram = jnp.concatenate([packed[:, COLS * q : COLS * (q + 1)] for q in range(4)], axis=0)
    row = lax.broadcasted_iota(jnp.int32, (COLS, COLS), 0)
    column = lax.broadcasted_iota(jnp.int32, (COLS, COLS), 1)
    work = jnp.concatenate([gram, jnp.where(row == column, 1.0, 0.0)], axis=1)
    wide_row = lax.broadcasted_iota(jnp.int32, work.shape, 0)
    for k in range(COLS):
        pivot = work[k : k + 1, k : k + 1]
        scale = 1.0 / jnp.sqrt(pivot)
        scaled = work[k : k + 1, :] * scale
        below = work[:, k : k + 1] * scale
        work = jnp.where(
            wide_row > k, work - below * scaled, jnp.where(wide_row == k, scaled, work)
        )
    factor_ref[...] = jnp.where(column >= row, work[:, :COLS], 0.0)
    basis_ref[...] = jnp.dot(
        work[:, COLS:], sketch_ref[...], precision=HIGH, preferred_element_type=F32
    )


def exchange(values, axes, capacity):
    slots = values.shape[0]
    parts = values.reshape(slots // capacity, capacity, LANES)
    parts = lax.all_to_all(parts, axes, split_axis=0, concat_axis=0, tiled=True)
    return parts.reshape(slots, LANES)


def on_device(omega, u_blocks, w_blocks, v_inverse, obs_camera, obs_track, obs_mask):
    track_count = lax.axis_size(TRACK)
    cam_count = lax.axis_size(CAM)
    devices = track_count * cam_count
    columns, params, cam_width = omega.shape
    obs = obs_camera.shape[0]
    capacity = max(2, 2 * obs // devices)
    slots = devices * capacity
    tracks = obs // BLK_OBS * TRK_BLK

    request, slot = call(
        functools.partial(request_kernel, capacity),
        (((slots, LANES), BF16), ((1, obs), jnp.int32)),
        obs_camera.reshape(1, obs),
        obs_mask.reshape(1, obs),
        w_blocks,
        scratch=(pltpu.VMEM((LANES, obs), F32),),
    )
    asked = exchange(request, TRACK_CAM, capacity)

    table = omega.transpose(1, 0, 2)
    wide_table = jnp.concatenate(
        [table, table, table, jnp.zeros((params, LANES - 3 * columns, cam_width), BF16)], axis=1
    ).reshape(params * LANES, cam_width)
    (reply,) = call(project_kernel, (((slots, LANES), BF16),), asked, wide_table)
    projected = exchange(reply, TRACK_CAM, capacity)

    by_track, by_slot = call(
        member_kernel,
        (((tracks, slots), BF16), ((slots, tracks), BF16)),
        slot,
        obs_track.reshape(1, obs),
    )
    (outgoing,) = call(
        solve_kernel, (((slots, LANES), BF16),), projected, by_track, by_slot, v_inverse
    )
    solved = exchange(outgoing, TRACK_CAM, capacity)

    weights, own = call(
        weights_kernel,
        (((3 * slots, params * cam_width), BF16), ((columns, params * cam_width), F32)),
        asked,
        table,
        u_blocks,
    )
    sketch, gram = call(
        sketch_kernel,
        (((columns, params * cam_width), F32), ((cam_count, 8, LANES), F32)),
        solved,
        weights,
        own,
    )
    gram = lax.all_to_all(gram, CAM, split_axis=0, concat_axis=0, tiled=True)
    (gram,) = call(gather_kernel, (((track_count, 8, LANES), F32),), gram)
    gram = lax.all_to_all(gram, TRACK, split_axis=0, concat_axis=0, tiled=True)
    basis, factor = call(
        functools.partial(finish_kernel, float(params * cam_width * devices)),
        (((columns, params * cam_width), F32), ((columns, columns), F32)),
        gram,
        sketch,
    )
    shape = (columns, params, cam_width)
    return (sketch.reshape(shape), basis.reshape(shape), factor)


def solution(mesh):
    track, cam = mesh.devices.shape
    split = Mesh(
        mesh.devices.reshape(8, track // 8, cam // 2, 2), ("track_0", "track_1", "cam_0", "cam_1")
    )
    return jax.shard_map(
        on_device,
        mesh=split,
        in_specs=(
            P(None, None, TRACK_CAM),
            P(None, None, TRACK_CAM),
            P(None, None, TRACK_CAM),
            P(None, None, TRACK_CAM),
            P(TRACK_CAM),
            P(TRACK_CAM),
            P(TRACK_CAM),
        ),
        out_specs=(P(None, None, TRACK_CAM), P(None, None, TRACK_CAM), P()),
        check_vma=False,
    )
```

```python
import functools

import jax
import jax.numpy as jnp
from jax import lax
from jax.experimental import pallas as pl
from jax.experimental.pallas import tpu as pltpu
from jax.sharding import Mesh
from jax.sharding import PartitionSpec as P

BLK_OBS = 128
TRK_BLK = 32
LANES = 128
PARAMS = 9
COLS = 32
TRACK = ("track_0", "track_1")
CAM = ("cam_0", "cam_1")
TRACK_CAM = TRACK + CAM
W_ROW = 3 * COLS
ID_ROW = W_ROW + 3 * PARAMS
HIGH = lax.Precision.HIGHEST
F32 = jnp.float32
BF16 = jnp.bfloat16


def dot_lanes(lhs, rhs):
    return lax.dot_general(lhs, rhs, (((1,), (1,)), ((), ())), preferred_element_type=F32)


def call(kernel, shapes, *args, scratch=(), in_specs=None):
    specs = {} if in_specs is None else {"in_specs": in_specs}
    return pl.pallas_call(
        kernel,
        out_shape=tuple(jax.ShapeDtypeStruct(s, d) for s, d in shapes),
        scratch_shapes=list(scratch),
        compiler_params=pltpu.CompilerParams(vmem_limit_bytes=32 << 20),
        **specs,
    )(*args)


def request_kernel(capacity, camera_hbm, mask_hbm, w_hbm, request_ref, slot_ref, camera_ref, mask_ref, w_ref, rows, sems):
    copies = [
        pltpu.make_async_copy(source, target, sems.at[n])
        for n, (source, target) in enumerate(
            ((camera_hbm, camera_ref), (mask_hbm, mask_ref), (w_hbm, w_ref))
        )
    ]
    for copy in copies:
        copy.start()
    rows[...] = jnp.zeros(rows.shape, F32)
    for copy in copies:
        copy.wait()
    obs = camera_ref.shape[1]
    camera = camera_ref[...]
    owner = lax.shift_right_logical(camera, 7)
    owner_f = owner.astype(F32)
    blocks = obs // LANES
    sub = lax.broadcasted_iota(jnp.int32, (LANES, LANES), 0)
    lane = lax.broadcasted_iota(jnp.int32, (LANES, LANES), 1)
    row_of = [owner_f[:, LANES * b : LANES * (b + 1)] for b in range(blocks)]
    column_of = [jnp.broadcast_to(r, (LANES, LANES)).T for r in row_of]
    ranks = []
    for q in range(blocks):
        same = jnp.where((column_of[q] == row_of[q]) & (sub < lane), 1.0, 0.0)
        for b in range(q):
            same = same + jnp.where(column_of[b] == row_of[q], 1.0, 0.0)
        ranks.append(jnp.sum(same, axis=0, keepdims=True))
    slot = owner * capacity + jnp.concatenate(ranks, axis=1).astype(jnp.int32)
    slot_ref[...] = slot
    live = mask_ref[...].astype(F32)
    for m in range(PARAMS):
        rows[W_ROW + 3 * m : W_ROW + 3 * m + 3, :] = w_ref[m].astype(F32) * live
    rows[ID_ROW : ID_ROW + 1, :] = (camera & (LANES - 1)).astype(F32)
    values = rows[...].astype(BF16)
    slots = request_ref.shape[0]
    step = 256
    for s in range(0, slots, step):
        ids = lax.broadcasted_iota(jnp.int32, (step, obs), 0) + s
        chosen = jnp.where(ids == slot, 1.0, 0.0).astype(BF16)
        request_ref[s : s + step, :] = dot_lanes(chosen, values).astype(BF16)


def member_kernel(slot_ref, track_ref, by_track_ref, by_slot_ref):
    obs = slot_ref.shape[1]
    tracks, slots = by_track_ref.shape
    position = lax.broadcasted_iota(jnp.int32, (1, obs), 1)
    track = lax.shift_right_logical(position, 7) * TRK_BLK + track_ref[...]
    ids = lax.broadcasted_iota(jnp.int32, (tracks, obs), 0)
    member = jnp.where(ids == track, 1.0, 0.0).astype(BF16)
    step = 256
    for s in range(0, slots, step):
        ids = lax.broadcasted_iota(jnp.int32, (step, obs), 0) + s
        chosen = jnp.where(ids == slot_ref[...], 1.0, 0.0).astype(BF16)
        by_track_ref[:, s : s + step] = dot_lanes(member, chosen).astype(BF16)
        by_slot_ref[s : s + step, :] = dot_lanes(chosen, member).astype(BF16)


def dot(lhs, rhs):
    return jnp.dot(lhs, rhs, preferred_element_type=F32)


def project_kernel(capacity, request_ref, table_ref, reply_ref, rows, out_rows):
    cams = table_ref.shape[0]
    slots = request_ref.shape[0]
    tracks = slots // (cams * capacity)
    rows[...] = request_ref[...].astype(F32)
    for b in range(cams):
        places = [pl.ds(b * capacity + r, tracks, stride=cams * capacity) for r in range(capacity)]
        turned = jnp.concatenate([rows[p, :] for p in places], axis=0).T
        wanted = lax.broadcasted_iota(jnp.int32, turned.shape, 0).astype(F32)
        chosen = jnp.where(wanted == turned[ID_ROW : ID_ROW + 1, :], 1.0, 0.0).astype(BF16)
        found = dot(table_ref[b], chosen)
        parts = []
        for i in range(3):
            part = jnp.zeros((COLS, turned.shape[1]), F32)
            for m in range(PARAMS):
                w_row = W_ROW + 3 * m + i
                part = part + turned[w_row : w_row + 1, :] * found[COLS * m : COLS * (m + 1), :]
            parts.append(part)
        parts.append(jnp.zeros((LANES - 3 * COLS, turned.shape[1]), F32))
        projected = jnp.concatenate(parts, axis=0).T
        for r, place in enumerate(places):
            out_rows[place, :] = projected[r * tracks : (r + 1) * tracks, :]
    reply_ref[...] = out_rows[...].astype(BF16)


def solve_kernel(reply_ref, by_track_ref, by_slot_ref, v_ref, request_ref, out_ref):
    summed = dot(by_track_ref[...], reply_ref[...]).T
    parts = []
    for i in range(3):
        part = jnp.zeros((COLS, LANES), F32)
        for k in range(3):
            part = part + v_ref[i, k : k + 1, :] * summed[COLS * k : COLS * (k + 1), :]
        parts.append(part)
    parts.append(jnp.zeros((LANES - 3 * COLS, LANES), F32))
    solved = jnp.concatenate(parts, axis=0).astype(BF16)
    spread = dot_lanes(by_slot_ref[...], solved).astype(BF16)
    lane = lax.broadcasted_iota(jnp.int32, spread.shape, 1)
    out_ref[...] = jnp.where(lane < W_ROW, spread, request_ref[...])


def own_kernel(omega_ref, u_ref, own_ref):
    table = [omega_ref[n].astype(F32) for n in range(PARAMS)]
    for m in range(PARAMS):
        total = jnp.zeros(table[0].shape, F32)
        for n in range(PARAMS):
            total = total + u_ref[m, n : n + 1, :] * table[n]
        own_ref[m] = total


def sketch_kernel(solved_ref, own_ref, sketch_ref, gram_ref):
    turned = solved_ref[...].astype(F32).T
    wanted = lax.broadcasted_iota(jnp.int32, turned.shape, 0).astype(F32)
    chosen = jnp.where(wanted == turned[ID_ROW : ID_ROW + 1, :], 1.0, 0.0).astype(BF16)
    tops, rests = [], []
    for m in range(PARAMS):
        part = jnp.zeros((COLS, turned.shape[1]), F32)
        for i in range(3):
            w_row = W_ROW + 3 * m + i
            part = part + turned[w_row : w_row + 1, :] * turned[COLS * i : COLS * (i + 1), :]
        top = part.astype(BF16)
        tops.append(top)
        rests.append((part - top.astype(F32)).astype(BF16))
    summed = dot_lanes(jnp.concatenate(tops + rests, axis=0), chosen)
    half = PARAMS * COLS
    parts = []
    for m in range(PARAMS):
        at = COLS * m
        parts.append(own_ref[m] - (summed[at : at + COLS, :] + summed[half + at : half + at + COLS, :]))
        sketch_ref[m] = parts[m]
    wide = jnp.concatenate(parts, axis=1)
    gram = lax.dot_general(
        wide, wide, (((1,), (1,)), ((), ())), precision=HIGH, preferred_element_type=F32
    )
    packed = jnp.concatenate([gram[8 * q : 8 * q + 8, :] for q in range(4)], axis=1)
    gram_ref[...] = jnp.broadcast_to(packed[None], gram_ref.shape)


def gather_kernel(parts_ref, out_ref):
    out_ref[...] = jnp.broadcast_to(jnp.sum(parts_ref[...], axis=0)[None], out_ref.shape)


def finish_kernel(row_total, parts_ref, sketch_ref, basis_ref, factor_ref):
    packed = jnp.sum(parts_ref[...], axis=0) / row_total
    gram = jnp.concatenate([packed[:, COLS * q : COLS * (q + 1)] for q in range(4)], axis=0)
    row = lax.broadcasted_iota(jnp.int32, (COLS, COLS), 0)
    column = lax.broadcasted_iota(jnp.int32, (COLS, COLS), 1)
    work = jnp.concatenate([gram, jnp.where(row == column, 1.0, 0.0)], axis=1)
    wide_row = lax.broadcasted_iota(jnp.int32, work.shape, 0)
    for k in range(COLS):
        pivot = work[k : k + 1, k : k + 1]
        scale = 1.0 / jnp.sqrt(pivot)
        scaled = work[k : k + 1, :] * scale
        below = work[:, k : k + 1] * scale
        work = jnp.where(
            wide_row > k, work - below * scaled, jnp.where(wide_row == k, scaled, work)
        )
    factor_ref[...] = jnp.where(column >= row, work[:, :COLS], 0.0)
    wide = jnp.concatenate([sketch_ref[m] for m in range(PARAMS)], axis=1)
    basis = jnp.dot(work[:, COLS:], wide, precision=HIGH, preferred_element_type=F32)
    for m in range(PARAMS):
        basis_ref[m] = basis[:, LANES * m : LANES * (m + 1)]


def exchange(values, axes):
    peers = lax.axis_size(axes)
    parts = values.reshape(peers, values.shape[0] // peers, *values.shape[1:])
    parts = lax.all_to_all(parts, axes, split_axis=0, concat_axis=0, tiled=True)
    return parts.reshape(values.shape)


def on_device(omega, u_blocks, w_blocks, v_inverse, obs_camera, obs_track, obs_mask):
    track_count = lax.axis_size(TRACK)
    cam_count = lax.axis_size(CAM)
    devices = track_count * cam_count
    columns, params, cam_width = omega.shape
    obs = obs_camera.shape[0]
    capacity = max(2, 2 * obs // devices)
    slots = devices * capacity
    tracks = obs // BLK_OBS * TRK_BLK
    by_slot_shape = ((slots, LANES), BF16)

    table = omega.transpose(1, 0, 2)
    row_table = lax.all_gather(table.reshape(params * columns, cam_width), CAM)

    request, slot = call(
        functools.partial(request_kernel, capacity),
        (by_slot_shape, ((1, obs), jnp.int32)),
        obs_camera.reshape(1, obs),
        obs_mask.reshape(1, obs),
        w_blocks,
        scratch=(
            pltpu.VMEM((1, obs), jnp.int32),
            pltpu.VMEM((1, obs), jnp.int32),
            pltpu.VMEM(w_blocks.shape, BF16),
            pltpu.VMEM((LANES, obs), F32),
            pltpu.SemaphoreType.DMA((3,)),
        ),
        in_specs=[pl.BlockSpec(memory_space=pl.ANY)] * 3,
    )
    asked = exchange(request, TRACK)
    (reply,) = call(
        functools.partial(project_kernel, capacity),
        (by_slot_shape,),
        asked,
        row_table,
        scratch=(pltpu.VMEM((slots, LANES), F32), pltpu.VMEM((slots, LANES), F32)),
    )
    projected = exchange(reply, TRACK)

    by_track, by_slot = call(
        member_kernel,
        (((tracks, slots), BF16), ((slots, tracks), BF16)),
        slot,
        obs_track.reshape(1, obs),
    )
    (outgoing,) = call(
        solve_kernel, (by_slot_shape,), projected, by_track, by_slot, v_inverse, request
    )
    solved = exchange(outgoing, TRACK_CAM)

    sketch_shape = ((params, columns, cam_width), F32)
    (own,) = call(own_kernel, (sketch_shape,), table, u_blocks)
    sketch, gram = call(
        sketch_kernel, (sketch_shape, ((cam_count, 8, LANES), F32)), solved, own
    )
    gram = lax.all_to_all(gram, CAM, split_axis=0, concat_axis=0, tiled=True)
    (gram,) = call(gather_kernel, (((track_count, 8, LANES), F32),), gram)
    gram = lax.all_to_all(gram, TRACK, split_axis=0, concat_axis=0, tiled=True)
    basis, factor = call(
        functools.partial(finish_kernel, float(params * cam_width * devices)),
        (sketch_shape, ((columns, columns), F32)),
        gram,
        sketch,
    )
    return (sketch.transpose(1, 0, 2), basis.transpose(1, 0, 2), factor)


def solution(mesh):
    track, cam = mesh.devices.shape
    split = Mesh(
        mesh.devices.reshape(8, track // 8, cam // 2, 2), ("track_0", "track_1", "cam_0", "cam_1")
    )
    return jax.shard_map(
        on_device,
        mesh=split,
        in_specs=(
            P(None, None, TRACK_CAM),
            P(None, None, TRACK_CAM),
            P(None, None, TRACK_CAM),
            P(None, None, TRACK_CAM),
            P(TRACK_CAM),
            P(TRACK_CAM),
            P(TRACK_CAM),
        ),
        out_specs=(P(None, None, TRACK_CAM), P(None, None, TRACK_CAM), P()),
        check_vma=False,
    )
```

```python
import functools

import jax
import jax.numpy as jnp
from jax import lax
from jax.experimental import pallas as pl
from jax.experimental.pallas import tpu as pltpu
from jax.sharding import Mesh
from jax.sharding import PartitionSpec as P

BLK_OBS = 128
TRK_BLK = 32
LANES = 128
PARAMS = 9
COLS = 32
TRACK = ("track_0", "track_1")
CAM = ("cam_0", "cam_1")
TRACK_CAM = TRACK + CAM
FIRST = ("track_1", "cam_1")
SECOND = ("track_0", "cam_0")
W_ROW = 3 * COLS
ID_ROW = W_ROW + 3 * PARAMS
HIGH = lax.Precision.HIGHEST
F32 = jnp.float32
BF16 = jnp.bfloat16


def dot_lanes(lhs, rhs):
    return lax.dot_general(lhs, rhs, (((1,), (1,)), ((), ())), preferred_element_type=F32)


def call(kernel, shapes, *args, scratch=(), in_specs=None):
    specs = {} if in_specs is None else {"in_specs": in_specs}
    return pl.pallas_call(
        kernel,
        out_shape=tuple(jax.ShapeDtypeStruct(s, d) for s, d in shapes),
        scratch_shapes=list(scratch),
        compiler_params=pltpu.CompilerParams(vmem_limit_bytes=32 << 20),
        **specs,
    )(*args)


def request_kernel(
    capacity,
    camera_hbm,
    mask_hbm,
    w_hbm,
    request_ref,
    slot_ref,
    values_ref,
    camera_ref,
    mask_ref,
    w_ref,
    rows,
    sems,
):
    copies = [
        pltpu.make_async_copy(source, target, sems.at[n])
        for n, (source, target) in enumerate(
            ((camera_hbm, camera_ref), (mask_hbm, mask_ref), (w_hbm, w_ref))
        )
    ]
    for copy in copies:
        copy.start()
    rows[...] = jnp.zeros(rows.shape, F32)
    for copy in copies:
        copy.wait()
    obs = camera_ref.shape[1]
    camera = camera_ref[...]
    owner = lax.shift_right_logical(camera, 7)
    owner_f = owner.astype(F32)
    blocks = obs // LANES
    sub = lax.broadcasted_iota(jnp.int32, (LANES, LANES), 0)
    lane = lax.broadcasted_iota(jnp.int32, (LANES, LANES), 1)
    row_of = [owner_f[:, LANES * b : LANES * (b + 1)] for b in range(blocks)]
    column_of = [jnp.broadcast_to(r, (LANES, LANES)).T for r in row_of]
    ranks = []
    for q in range(blocks):
        same = jnp.where((column_of[q] == row_of[q]) & (sub < lane), 1.0, 0.0)
        for b in range(q):
            same = same + jnp.where(column_of[b] == row_of[q], 1.0, 0.0)
        ranks.append(jnp.sum(same, axis=0, keepdims=True))
    slot = owner * capacity + jnp.concatenate(ranks, axis=1).astype(jnp.int32)
    slot_ref[...] = slot
    live = mask_ref[...].astype(F32)
    for m in range(PARAMS):
        rows[W_ROW + 3 * m : W_ROW + 3 * m + 3, :] = w_ref[m].astype(F32) * live
    rows[ID_ROW : ID_ROW + 1, :] = (camera & (LANES - 1)).astype(F32)
    values = rows[...].astype(BF16)
    values_ref[...] = values
    slots = request_ref.shape[0]
    step = 256
    for s in range(0, slots, step):
        ids = lax.broadcasted_iota(jnp.int32, (step, obs), 0) + s
        chosen = jnp.where(ids == slot, 1.0, 0.0).astype(BF16)
        request_ref[s : s + step, :] = dot_lanes(chosen, values).astype(BF16)


def member_kernel(slot_ref, track_ref, values_ref, by_track_ref, by_slot_ref, base_ref):
    obs = slot_ref.shape[1]
    tracks, slots = by_track_ref.shape
    position = lax.broadcasted_iota(jnp.int32, (1, obs), 1)
    track = lax.shift_right_logical(position, 7) * TRK_BLK + track_ref[...]
    ids = lax.broadcasted_iota(jnp.int32, (tracks, obs), 0)
    member = jnp.where(ids == track, 1.0, 0.0).astype(BF16)
    step = 256
    for s in range(0, slots, step):
        ids = lax.broadcasted_iota(jnp.int32, (step, obs), 0) + s
        chosen = jnp.where(ids == slot_ref[...], 1.0, 0.0).astype(BF16)
        by_track_ref[:, s : s + step] = dot_lanes(member, chosen).astype(BF16)
        by_slot_ref[s : s + step, :] = dot_lanes(chosen, member).astype(BF16)
        base_ref[s : s + step, :] = dot_lanes(chosen, values_ref[...]).astype(BF16)


def dot(lhs, rhs):
    return jnp.dot(lhs, rhs, preferred_element_type=F32)


def project_kernel(capacity, request_ref, table_ref, reply_ref, rows, out_rows):
    cams = table_ref.shape[0]
    slots = request_ref.shape[0]
    tracks = slots // (cams * capacity)
    rows[...] = request_ref[...].astype(F32)
    for b in range(cams):
        places = [pl.ds(b * capacity + r, tracks, stride=cams * capacity) for r in range(capacity)]
        turned = jnp.concatenate([rows[p, :] for p in places], axis=0).T
        wanted = lax.broadcasted_iota(jnp.int32, turned.shape, 0).astype(F32)
        chosen = jnp.where(wanted == turned[ID_ROW : ID_ROW + 1, :], 1.0, 0.0).astype(BF16)
        found = dot(table_ref[b], chosen)
        parts = []
        for i in range(3):
            part = jnp.zeros((COLS, turned.shape[1]), F32)
            for m in range(PARAMS):
                w_row = W_ROW + 3 * m + i
                part = part + turned[w_row : w_row + 1, :] * found[COLS * m : COLS * (m + 1), :]
            parts.append(part)
        parts.append(jnp.zeros((LANES - 3 * COLS, turned.shape[1]), F32))
        projected = jnp.concatenate(parts, axis=0).T
        for r, place in enumerate(places):
            out_rows[place, :] = projected[r * tracks : (r + 1) * tracks, :]
    reply_ref[...] = out_rows[...].astype(BF16)


def solve_kernel(reply_ref, by_track_ref, by_slot_ref, v_ref, base_ref, out_ref):
    summed = dot(by_track_ref[...], reply_ref[...]).T
    parts = []
    for i in range(3):
        part = jnp.zeros((COLS, LANES), F32)
        for k in range(3):
            part = part + v_ref[i, k : k + 1, :] * summed[COLS * k : COLS * (k + 1), :]
        parts.append(part)
    parts.append(jnp.zeros((LANES - 3 * COLS, LANES), F32))
    solved = jnp.concatenate(parts, axis=0).astype(BF16)
    spread = dot_lanes(by_slot_ref[...], solved).astype(BF16)
    lane = lax.broadcasted_iota(jnp.int32, spread.shape, 1)
    out_ref[...] = jnp.where(lane < W_ROW, spread, base_ref[...])


def own_kernel(omega_ref, u_ref, own_ref):
    table = [omega_ref[n].astype(F32) for n in range(PARAMS)]
    for m in range(PARAMS):
        total = jnp.zeros(table[0].shape, F32)
        for n in range(PARAMS):
            total = total + u_ref[m, n : n + 1, :] * table[n]
        own_ref[m] = total


def sketch_kernel(solved_ref, own_ref, sketch_ref, gram_ref):
    turned = solved_ref[...].astype(F32).T
    wanted = lax.broadcasted_iota(jnp.int32, turned.shape, 0).astype(F32)
    chosen = jnp.where(wanted == turned[ID_ROW : ID_ROW + 1, :], 1.0, 0.0).astype(BF16)
    tops, rests = [], []
    for m in range(PARAMS):
        part = jnp.zeros((COLS, turned.shape[1]), F32)
        for i in range(3):
            w_row = W_ROW + 3 * m + i
            part = part + turned[w_row : w_row + 1, :] * turned[COLS * i : COLS * (i + 1), :]
        top = part.astype(BF16)
        tops.append(top)
        rests.append((part - top.astype(F32)).astype(BF16))
    summed = dot_lanes(jnp.concatenate(tops + rests, axis=0), chosen)
    half = PARAMS * COLS
    parts = []
    for m in range(PARAMS):
        at = COLS * m
        parts.append(own_ref[m] - (summed[at : at + COLS, :] + summed[half + at : half + at + COLS, :]))
        sketch_ref[m] = parts[m]
    wide = jnp.concatenate(parts, axis=1)
    gram = lax.dot_general(
        wide, wide, (((1,), (1,)), ((), ())), precision=HIGH, preferred_element_type=F32
    )
    packed = jnp.concatenate([gram[8 * q : 8 * q + 8, :] for q in range(4)], axis=1)
    gram_ref[...] = jnp.broadcast_to(packed[None], gram_ref.shape)


def gather_kernel(parts_ref, out_ref):
    out_ref[...] = jnp.broadcast_to(jnp.sum(parts_ref[...], axis=0)[None], out_ref.shape)


def finish_kernel(row_total, parts_ref, sketch_ref, basis_ref, factor_ref):
    packed = jnp.sum(parts_ref[...], axis=0) / row_total
    gram = jnp.concatenate([packed[:, COLS * q : COLS * (q + 1)] for q in range(4)], axis=0)
    row = lax.broadcasted_iota(jnp.int32, (COLS, COLS), 0)
    column = lax.broadcasted_iota(jnp.int32, (COLS, COLS), 1)
    work = jnp.concatenate([gram, jnp.where(row == column, 1.0, 0.0)], axis=1)
    wide_row = lax.broadcasted_iota(jnp.int32, work.shape, 0)
    for k in range(COLS):
        pivot = work[k : k + 1, k : k + 1]
        scale = 1.0 / jnp.sqrt(pivot)
        scaled = work[k : k + 1, :] * scale
        below = work[:, k : k + 1] * scale
        work = jnp.where(
            wide_row > k, work - below * scaled, jnp.where(wide_row == k, scaled, work)
        )
    factor_ref[...] = jnp.where(column >= row, work[:, :COLS], 0.0)
    wide = jnp.concatenate([sketch_ref[m] for m in range(PARAMS)], axis=1)
    basis = jnp.dot(work[:, COLS:], wide, precision=HIGH, preferred_element_type=F32)
    for m in range(PARAMS):
        basis_ref[m] = basis[:, LANES * m : LANES * (m + 1)]


def exchange(values, axes):
    peers = lax.axis_size(axes)
    parts = values.reshape(peers, values.shape[0] // peers, *values.shape[1:])
    parts = lax.all_to_all(parts, axes, split_axis=0, concat_axis=0, tiled=True)
    return parts.reshape(values.shape)


def on_device(omega, u_blocks, w_blocks, v_inverse, obs_camera, obs_track, obs_mask):
    track_count = lax.axis_size(TRACK)
    cam_count = lax.axis_size(CAM)
    devices = track_count * cam_count
    columns, params, cam_width = omega.shape
    obs = obs_camera.shape[0]
    capacity = max(2, 2 * obs // devices)
    slots = devices * capacity
    tracks = obs // BLK_OBS * TRK_BLK
    by_slot_shape = ((slots, LANES), BF16)

    table = omega.transpose(1, 0, 2)
    tables = lax.all_gather(table.reshape(params * columns, cam_width), CAM)

    request, slot, values = call(
        functools.partial(request_kernel, capacity),
        (by_slot_shape, ((1, obs), jnp.int32), ((LANES, obs), BF16)),
        *(
            pltpu.with_memory_space_constraint(x, pltpu.HBM)
            for x in (obs_camera.reshape(1, obs), obs_mask.reshape(1, obs), w_blocks)
        ),
        scratch=(
            pltpu.VMEM((1, obs), jnp.int32),
            pltpu.VMEM((1, obs), jnp.int32),
            pltpu.VMEM(w_blocks.shape, BF16),
            pltpu.VMEM((LANES, obs), F32),
            pltpu.SemaphoreType.DMA((3,)),
        ),
        in_specs=[pl.BlockSpec(memory_space=pltpu.HBM)] * 3,
    )
    asked = exchange(request, TRACK)
    (reply,) = call(
        functools.partial(project_kernel, capacity),
        (by_slot_shape,),
        asked,
        tables,
        scratch=(pltpu.VMEM((slots, LANES), F32), pltpu.VMEM((slots, LANES), F32)),
    )
    projected = exchange(reply, TRACK)

    by_track, by_slot, base = call(
        member_kernel,
        (((tracks, slots), BF16), ((slots, tracks), BF16), by_slot_shape),
        slot,
        obs_track.reshape(1, obs),
        values,
    )
    (outgoing,) = call(
        solve_kernel, (by_slot_shape,), projected, by_track, by_slot, v_inverse, base
    )
    solved = exchange(outgoing, TRACK_CAM)

    sketch_shape = ((params, columns, cam_width), F32)
    (own,) = call(own_kernel, (sketch_shape,), table, u_blocks)
    sketch, gram = call(
        sketch_kernel, (sketch_shape, ((lax.axis_size(FIRST), 8, LANES), F32)), solved, own
    )
    gram = lax.all_to_all(gram, FIRST, split_axis=0, concat_axis=0, tiled=True)
    (gram,) = call(gather_kernel, (((lax.axis_size(SECOND), 8, LANES), F32),), gram)
    gram = lax.all_to_all(gram, SECOND, split_axis=0, concat_axis=0, tiled=True)
    basis, factor = call(
        functools.partial(finish_kernel, float(params * cam_width * devices)),
        (sketch_shape, ((columns, columns), F32)),
        gram,
        sketch,
    )
    return (sketch.transpose(1, 0, 2), basis.transpose(1, 0, 2), factor)


def solution(mesh):
    track, cam = mesh.devices.shape
    split = Mesh(
        mesh.devices.reshape(8, track // 8, cam // 2, 2), ("track_0", "track_1", "cam_0", "cam_1")
    )
    return jax.shard_map(
        on_device,
        mesh=split,
        in_specs=(
            P(None, None, TRACK_CAM),
            P(None, None, TRACK_CAM),
            P(None, None, TRACK_CAM),
            P(None, None, TRACK_CAM),
            P(TRACK_CAM),
            P(TRACK_CAM),
            P(TRACK_CAM),
        ),
        out_specs=(P(None, None, TRACK_CAM), P(None, None, TRACK_CAM), P()),
        check_vma=False,
    )
```

```python
import functools

import jax
import jax.numpy as jnp
from jax import lax
from jax.experimental import pallas as pl
from jax.experimental.pallas import tpu as pltpu
from jax.sharding import Mesh
from jax.sharding import PartitionSpec as P

BLK_OBS = 128
TRK_BLK = 32
LANES = 128
PARAMS = 9
COLS = 32
TRACK = ("track_0", "track_1")
CAM = ("cam_0", "cam_1")
TRACK_CAM = TRACK + CAM
FIRST = ("track_1", "cam_1")
SECOND = ("track_0", "cam_0")
W_ROW = 3 * COLS
ID_ROW = W_ROW + 3 * PARAMS
HIGH = lax.Precision.HIGHEST
F32 = jnp.float32
BF16 = jnp.bfloat16


def dot_lanes(lhs, rhs):
    return lax.dot_general(lhs, rhs, (((1,), (1,)), ((), ())), preferred_element_type=F32)


def call(kernel, shapes, *args, scratch=(), in_specs=None):
    specs = {} if in_specs is None else {"in_specs": in_specs}
    return pl.pallas_call(
        kernel,
        out_shape=tuple(jax.ShapeDtypeStruct(s, d) for s, d in shapes),
        scratch_shapes=list(scratch),
        compiler_params=pltpu.CompilerParams(vmem_limit_bytes=32 << 20),
        **specs,
    )(*args)


def request_kernel(
    sizes,
    camera_hbm,
    mask_hbm,
    w_hbm,
    request_ref,
    slot_ref,
    values_ref,
    camera_ref,
    mask_ref,
    w_ref,
    rows,
    sems,
):
    capacity, head, block = sizes
    copies = [
        pltpu.make_async_copy(source, target, sems.at[n])
        for n, (source, target) in enumerate(
            ((camera_hbm, camera_ref), (mask_hbm, mask_ref), (w_hbm, w_ref))
        )
    ]
    for copy in copies:
        copy.start()
    rows[...] = jnp.zeros(rows.shape, F32)
    for copy in copies:
        copy.wait()
    obs = camera_ref.shape[1]
    camera = camera_ref[...]
    owner = lax.shift_right_logical(camera, 7)
    owner_f = owner.astype(F32)
    blocks = obs // LANES
    sub = lax.broadcasted_iota(jnp.int32, (LANES, LANES), 0)
    lane = lax.broadcasted_iota(jnp.int32, (LANES, LANES), 1)
    row_of = [owner_f[:, LANES * b : LANES * (b + 1)] for b in range(blocks)]
    column_of = [jnp.broadcast_to(r, (LANES, LANES)).T for r in row_of]
    ranks = []
    for q in range(blocks):
        same = jnp.where((column_of[q] == row_of[q]) & (sub < lane), 1.0, 0.0)
        for b in range(q):
            same = same + jnp.where(column_of[b] == row_of[q], 1.0, 0.0)
        ranks.append(jnp.sum(same, axis=0, keepdims=True))
    slot = owner * capacity + jnp.concatenate(ranks, axis=1).astype(jnp.int32)
    slot_ref[...] = slot
    at_head = (slot >= head) & (slot < head + block)
    slot = jnp.where(slot < block, slot + head, jnp.where(at_head, slot - head, slot))
    live = mask_ref[...].astype(F32)
    for m in range(PARAMS):
        rows[W_ROW + 3 * m : W_ROW + 3 * m + 3, :] = w_ref[m].astype(F32) * live
    rows[ID_ROW : ID_ROW + 1, :] = (camera & (LANES - 1)).astype(F32)
    values = rows[...].astype(BF16)
    values_ref[...] = values
    slots = request_ref.shape[0]
    step = 256
    for s in range(0, slots, step):
        ids = lax.broadcasted_iota(jnp.int32, (step, obs), 0) + s
        chosen = jnp.where(ids == slot, 1.0, 0.0).astype(BF16)
        request_ref[s : s + step, :] = dot_lanes(chosen, values).astype(BF16)


def member_kernel(slot_ref, track_ref, values_ref, by_track_ref, by_slot_ref, base_ref):
    obs = slot_ref.shape[1]
    tracks, slots = by_track_ref.shape
    position = lax.broadcasted_iota(jnp.int32, (1, obs), 1)
    track = lax.shift_right_logical(position, 7) * TRK_BLK + track_ref[...]
    ids = lax.broadcasted_iota(jnp.int32, (tracks, obs), 0)
    member = jnp.where(ids == track, 1.0, 0.0).astype(BF16)
    step = 256
    for s in range(0, slots, step):
        ids = lax.broadcasted_iota(jnp.int32, (step, obs), 0) + s
        chosen = jnp.where(ids == slot_ref[...], 1.0, 0.0).astype(BF16)
        by_track_ref[:, s : s + step] = dot_lanes(member, chosen).astype(BF16)
        by_slot_ref[s : s + step, :] = dot_lanes(chosen, member).astype(BF16)
        base_ref[s : s + step, :] = dot_lanes(chosen, values_ref[...]).astype(BF16)


def dot(lhs, rhs):
    return jnp.dot(lhs, rhs, preferred_element_type=F32)


def project_kernel(sizes, request_ref, table_ref, reply_ref, rows, out_rows):
    capacity, head, block = sizes
    cams = table_ref.shape[0]
    slots = request_ref.shape[0]
    tracks = slots // (cams * capacity)
    rows[...] = request_ref[...].astype(F32)
    for b in range(cams):
        places = [pl.ds(b * capacity + r, tracks, stride=cams * capacity) for r in range(capacity)]
        turned = jnp.concatenate([rows[p, :] for p in places], axis=0).T
        wanted = lax.broadcasted_iota(jnp.int32, turned.shape, 0).astype(F32)
        chosen = jnp.where(wanted == turned[ID_ROW : ID_ROW + 1, :], 1.0, 0.0).astype(BF16)
        found = dot(table_ref[b], chosen)
        parts = []
        for i in range(3):
            part = jnp.zeros((COLS, turned.shape[1]), F32)
            for m in range(PARAMS):
                w_row = W_ROW + 3 * m + i
                part = part + turned[w_row : w_row + 1, :] * found[COLS * m : COLS * (m + 1), :]
            parts.append(part)
        parts.append(jnp.zeros((LANES - 3 * COLS, turned.shape[1]), F32))
        projected = jnp.concatenate(parts, axis=0).T
        for r, place in enumerate(places):
            out_rows[place, :] = projected[r * tracks : (r + 1) * tracks, :]
    reply_ref[...] = out_rows[...].astype(BF16)
    reply_ref[0:block, :] = out_rows[head : head + block, :].astype(BF16)
    reply_ref[head : head + block, :] = out_rows[0:block, :].astype(BF16)


def solve_kernel(reply_ref, by_track_ref, by_slot_ref, v_ref, base_ref, out_ref):
    summed = dot(by_track_ref[...], reply_ref[...]).T
    parts = []
    for i in range(3):
        part = jnp.zeros((COLS, LANES), F32)
        for k in range(3):
            part = part + v_ref[i, k : k + 1, :] * summed[COLS * k : COLS * (k + 1), :]
        parts.append(part)
    parts.append(jnp.zeros((LANES - 3 * COLS, LANES), F32))
    solved = jnp.concatenate(parts, axis=0).astype(BF16)
    spread = dot_lanes(by_slot_ref[...], solved).astype(BF16)
    lane = lax.broadcasted_iota(jnp.int32, spread.shape, 1)
    out_ref[...] = jnp.where(lane < W_ROW, spread, base_ref[...])


def own_kernel(omega_ref, u_ref, own_ref):
    table = [omega_ref[n].astype(F32) for n in range(PARAMS)]
    for m in range(PARAMS):
        total = jnp.zeros(table[0].shape, F32)
        for n in range(PARAMS):
            total = total + u_ref[m, n : n + 1, :] * table[n]
        own_ref[m] = total


def sketch_kernel(solved_ref, own_ref, sketch_ref, gram_ref):
    turned = solved_ref[...].astype(F32).T
    wanted = lax.broadcasted_iota(jnp.int32, turned.shape, 0).astype(F32)
    chosen = jnp.where(wanted == turned[ID_ROW : ID_ROW + 1, :], 1.0, 0.0).astype(BF16)
    tops, rests = [], []
    for m in range(PARAMS):
        part = jnp.zeros((COLS, turned.shape[1]), F32)
        for i in range(3):
            w_row = W_ROW + 3 * m + i
            part = part + turned[w_row : w_row + 1, :] * turned[COLS * i : COLS * (i + 1), :]
        top = part.astype(BF16)
        tops.append(top)
        rests.append((part - top.astype(F32)).astype(BF16))
    summed = dot_lanes(jnp.concatenate(tops + rests, axis=0), chosen)
    half = PARAMS * COLS
    parts = []
    for m in range(PARAMS):
        at = COLS * m
        parts.append(own_ref[m] - (summed[at : at + COLS, :] + summed[half + at : half + at + COLS, :]))
        sketch_ref[m] = parts[m]
    wide = jnp.concatenate(parts, axis=1)
    gram = lax.dot_general(
        wide, wide, (((1,), (1,)), ((), ())), precision=HIGH, preferred_element_type=F32
    )
    packed = jnp.concatenate([gram[8 * q : 8 * q + 8, :] for q in range(4)], axis=1)
    gram_ref[...] = jnp.broadcast_to(packed[None], gram_ref.shape)


def gather_kernel(parts_ref, out_ref):
    out_ref[...] = jnp.broadcast_to(jnp.sum(parts_ref[...], axis=0)[None], out_ref.shape)


def finish_kernel(row_total, parts_ref, sketch_ref, basis_ref, factor_ref):
    packed = jnp.sum(parts_ref[...], axis=0) / row_total
    gram = jnp.concatenate([packed[:, COLS * q : COLS * (q + 1)] for q in range(4)], axis=0)
    row = lax.broadcasted_iota(jnp.int32, (COLS, COLS), 0)
    column = lax.broadcasted_iota(jnp.int32, (COLS, COLS), 1)
    work = jnp.concatenate([gram, jnp.where(row == column, 1.0, 0.0)], axis=1)
    wide_row = lax.broadcasted_iota(jnp.int32, work.shape, 0)
    pivots = jnp.broadcast_to(work[:, 0:1], work.shape)
    for k in range(COLS - 1):
        ahead = jnp.broadcast_to(work[:, k + 1 : k + 2], work.shape)
        below = jnp.where(wide_row > k, pivots, 0.0) * (1.0 / pivots[k : k + 1, :])
        pivots = ahead - below * pivots[k + 1 : k + 2, :]
        work = work - below * work[k : k + 1, :]
    diagonal = jnp.sum(jnp.where(row == column, work[:, :COLS], 0.0), axis=1, keepdims=True)
    work = work * (1.0 / jnp.sqrt(diagonal))
    factor_ref[...] = jnp.where(column >= row, work[:, :COLS], 0.0)
    wide = jnp.concatenate([sketch_ref[m] for m in range(PARAMS)], axis=1)
    basis = jnp.dot(work[:, COLS:], wide, precision=HIGH, preferred_element_type=F32)
    for m in range(PARAMS):
        basis_ref[m] = basis[:, LANES * m : LANES * (m + 1)]


def middle(axes):
    index = 0
    for axis in axes:
        size = lax.axis_size(axis)
        index = index * size + (size // 2 if size > 2 else 0)
    return index


def exchange(values, axes, first=0):
    peers = lax.axis_size(axes)
    parts = values.reshape(peers, values.shape[0] // peers, *values.shape[1:])
    order = list(range(peers))
    order[0], order[first] = first, 0
    parts = lax.all_to_all(
        parts,
        axes,
        split_axis=0,
        concat_axis=0,
        tiled=True,
        axis_index_groups=[order] if first else None,
    )
    return parts.reshape(values.shape)


def on_device(omega, u_blocks, w_blocks, v_inverse, obs_camera, obs_track, obs_mask):
    track_count = lax.axis_size(TRACK)
    cam_count = lax.axis_size(CAM)
    devices = track_count * cam_count
    columns, params, cam_width = omega.shape
    obs = obs_camera.shape[0]
    capacity = max(2, 2 * obs // devices)
    slots = devices * capacity
    tracks = obs // BLK_OBS * TRK_BLK
    by_slot_shape = ((slots, LANES), BF16)

    table = omega.transpose(1, 0, 2)
    tables = lax.all_gather(table.reshape(params * columns, cam_width), CAM)

    head = middle(TRACK)
    block = cam_count * capacity
    request, slot, values = call(
        functools.partial(request_kernel, (capacity, head * block, block)),
        (by_slot_shape, ((1, obs), jnp.int32), ((LANES, obs), BF16)),
        *(
            pltpu.with_memory_space_constraint(x, pltpu.HBM)
            for x in (obs_camera.reshape(1, obs), obs_mask.reshape(1, obs), w_blocks)
        ),
        scratch=(
            pltpu.VMEM((1, obs), jnp.int32),
            pltpu.VMEM((1, obs), jnp.int32),
            pltpu.VMEM(w_blocks.shape, BF16),
            pltpu.VMEM((LANES, obs), F32),
            pltpu.SemaphoreType.DMA((3,)),
        ),
        in_specs=[pl.BlockSpec(memory_space=pltpu.HBM)] * 3,
    )
    asked = exchange(request, TRACK, head)
    (reply,) = call(
        functools.partial(project_kernel, (capacity, head * block, block)),
        (by_slot_shape,),
        asked,
        tables,
        scratch=(pltpu.VMEM((slots, LANES), F32), pltpu.VMEM((slots, LANES), F32)),
    )
    projected = exchange(reply, TRACK)

    by_track, by_slot, base = call(
        member_kernel,
        (((tracks, slots), BF16), ((slots, tracks), BF16), by_slot_shape),
        slot,
        obs_track.reshape(1, obs),
        values,
    )
    (outgoing,) = call(
        solve_kernel, (by_slot_shape,), projected, by_track, by_slot, v_inverse, base
    )
    solved = exchange(outgoing, TRACK_CAM)

    sketch_shape = ((params, columns, cam_width), F32)
    (own,) = call(own_kernel, (sketch_shape,), table, u_blocks)
    sketch, gram = call(
        sketch_kernel, (sketch_shape, ((lax.axis_size(FIRST), 8, LANES), F32)), solved, own
    )
    gram = exchange(gram, FIRST, middle(FIRST))
    (gram,) = call(gather_kernel, (((lax.axis_size(SECOND), 8, LANES), F32),), gram)
    gram = exchange(gram, SECOND, middle(SECOND))
    basis, factor = call(
        functools.partial(finish_kernel, float(params * cam_width * devices)),
        (sketch_shape, ((columns, columns), F32)),
        gram,
        sketch,
    )
    return (sketch.transpose(1, 0, 2), basis.transpose(1, 0, 2), factor)


def solution(mesh):
    track, cam = mesh.devices.shape
    split = Mesh(
        mesh.devices.reshape(8, track // 8, cam // 2, 2), ("track_0", "track_1", "cam_0", "cam_1")
    )
    return jax.shard_map(
        on_device,
        mesh=split,
        in_specs=(
            P(None, None, TRACK_CAM),
            P(None, None, TRACK_CAM),
            P(None, None, TRACK_CAM),
            P(None, None, TRACK_CAM),
            P(TRACK_CAM),
            P(TRACK_CAM),
            P(TRACK_CAM),
        ),
        out_specs=(P(None, None, TRACK_CAM), P(None, None, TRACK_CAM), P()),
        check_vma=False,
    )
```

```python
import functools

import jax
import jax.numpy as jnp
from jax import lax
from jax.experimental import pallas as pl
from jax.experimental.pallas import tpu as pltpu
from jax.sharding import Mesh
from jax.sharding import PartitionSpec as P

BLK_OBS = 128
TRK_BLK = 32
LANES = 128
PARAMS = 9
COLS = 32
TRACK = ("track_0", "track_1")
CAM = ("cam_0", "cam_1")
TRACK_CAM = TRACK + CAM
FIRST = ("track_1", "cam_1")
SECOND = ("track_0", "cam_0")
W_ROW = 3 * COLS
ID_ROW = W_ROW + 3 * PARAMS
HIGH = lax.Precision.HIGHEST
F32 = jnp.float32
BF16 = jnp.bfloat16


def dot_lanes(lhs, rhs):
    return lax.dot_general(lhs, rhs, (((1,), (1,)), ((), ())), preferred_element_type=F32)


def call(kernel, shapes, *args, scratch=(), in_specs=None):
    specs = {} if in_specs is None else {"in_specs": in_specs}
    return pl.pallas_call(
        kernel,
        out_shape=tuple(jax.ShapeDtypeStruct(s, d) for s, d in shapes),
        scratch_shapes=list(scratch),
        compiler_params=pltpu.CompilerParams(vmem_limit_bytes=32 << 20),
        **specs,
    )(*args)


def request_kernel(
    sizes,
    camera_hbm,
    mask_hbm,
    w_hbm,
    request_ref,
    slot_ref,
    values_ref,
    camera_ref,
    mask_ref,
    w_ref,
    rows,
    sems,
):
    capacity, head, block = sizes
    copies = [
        pltpu.make_async_copy(source, target, sems.at[n])
        for n, (source, target) in enumerate(
            ((camera_hbm, camera_ref), (mask_hbm, mask_ref), (w_hbm, w_ref))
        )
    ]
    for copy in copies:
        copy.start()
    rows[...] = jnp.zeros(rows.shape, F32)
    for copy in copies:
        copy.wait()
    obs = camera_ref.shape[1]
    camera = camera_ref[...]
    owner = lax.shift_right_logical(camera, 7)
    owner_f = owner.astype(F32)
    blocks = obs // LANES
    sub = lax.broadcasted_iota(jnp.int32, (LANES, LANES), 0)
    lane = lax.broadcasted_iota(jnp.int32, (LANES, LANES), 1)
    row_of = [owner_f[:, LANES * b : LANES * (b + 1)] for b in range(blocks)]
    column_of = [jnp.broadcast_to(r, (LANES, LANES)).T for r in row_of]
    ranks = []
    for q in range(blocks):
        same = jnp.where((column_of[q] == row_of[q]) & (sub < lane), 1.0, 0.0)
        for b in range(q):
            same = same + jnp.where(column_of[b] == row_of[q], 1.0, 0.0)
        ranks.append(jnp.sum(same, axis=0, keepdims=True))
    slot = owner * capacity + jnp.concatenate(ranks, axis=1).astype(jnp.int32)
    slot_ref[...] = slot
    at_head = (slot >= head) & (slot < head + block)
    slot = jnp.where(slot < block, slot + head, jnp.where(at_head, slot - head, slot))
    live = mask_ref[...].astype(F32)
    for m in range(PARAMS):
        rows[W_ROW + 3 * m : W_ROW + 3 * m + 3, :] = w_ref[m].astype(F32) * live
    rows[ID_ROW : ID_ROW + 1, :] = (camera & (LANES - 1)).astype(F32)
    values = rows[...].astype(BF16)
    values_ref[...] = values
    slots = request_ref.shape[0]
    step = 256
    for s in range(0, slots, step):
        ids = lax.broadcasted_iota(jnp.int32, (step, obs), 0) + s
        chosen = jnp.where(ids == slot, 1.0, 0.0).astype(BF16)
        request_ref[s : s + step, :] = dot_lanes(chosen, values).astype(BF16)


def member_kernel(slot_ref, track_ref, values_ref, by_track_ref, by_slot_ref, base_ref):
    obs = slot_ref.shape[1]
    tracks, slots = by_track_ref.shape
    position = lax.broadcasted_iota(jnp.int32, (1, obs), 1)
    track = lax.shift_right_logical(position, 7) * TRK_BLK + track_ref[...]
    ids = lax.broadcasted_iota(jnp.int32, (tracks, obs), 0)
    member = jnp.where(ids == track, 1.0, 0.0).astype(BF16)
    step = 256
    for s in range(0, slots, step):
        ids = lax.broadcasted_iota(jnp.int32, (step, obs), 0) + s
        chosen = jnp.where(ids == slot_ref[...], 1.0, 0.0).astype(BF16)
        by_track_ref[:, s : s + step] = dot_lanes(member, chosen).astype(BF16)
        by_slot_ref[s : s + step, :] = dot_lanes(chosen, member).astype(BF16)
        base_ref[s : s + step, :] = dot_lanes(chosen, values_ref[...]).astype(BF16)


def dot(lhs, rhs):
    return jnp.dot(lhs, rhs, preferred_element_type=F32)


def project_kernel(sizes, request_ref, table_ref, reply_ref, rows, out_rows):
    capacity, head, block = sizes
    cams = table_ref.shape[0]
    slots = request_ref.shape[0]
    tracks = slots // (cams * capacity)
    rows[...] = request_ref[...].astype(F32)
    for b in range(cams):
        places = [pl.ds(b * capacity + r, tracks, stride=cams * capacity) for r in range(capacity)]
        turned = jnp.concatenate([rows[p, :] for p in places], axis=0).T
        wanted = lax.broadcasted_iota(jnp.int32, turned.shape, 0).astype(F32)
        chosen = jnp.where(wanted == turned[ID_ROW : ID_ROW + 1, :], 1.0, 0.0).astype(BF16)
        found = dot(table_ref[b], chosen)
        parts = []
        for i in range(3):
            part = jnp.zeros((COLS, turned.shape[1]), F32)
            for m in range(PARAMS):
                w_row = W_ROW + 3 * m + i
                part = part + turned[w_row : w_row + 1, :] * found[COLS * m : COLS * (m + 1), :]
            parts.append(part)
        parts.append(jnp.zeros((LANES - 3 * COLS, turned.shape[1]), F32))
        projected = jnp.concatenate(parts, axis=0).T
        for r, place in enumerate(places):
            out_rows[place, :] = projected[r * tracks : (r + 1) * tracks, :]
    reply_ref[...] = out_rows[...].astype(BF16)
    reply_ref[0:block, :] = out_rows[head : head + block, :].astype(BF16)
    reply_ref[head : head + block, :] = out_rows[0:block, :].astype(BF16)


def solve_kernel(reply_ref, by_track_ref, by_slot_ref, v_ref, base_ref, out_ref):
    summed = dot(by_track_ref[...], reply_ref[...]).T
    parts = []
    for i in range(3):
        part = jnp.zeros((COLS, LANES), F32)
        for k in range(3):
            part = part + v_ref[i, k : k + 1, :] * summed[COLS * k : COLS * (k + 1), :]
        parts.append(part)
    parts.append(jnp.zeros((LANES - 3 * COLS, LANES), F32))
    solved = jnp.concatenate(parts, axis=0).astype(BF16)
    spread = dot_lanes(by_slot_ref[...], solved).astype(BF16)
    lane = lax.broadcasted_iota(jnp.int32, spread.shape, 1)
    out_ref[...] = jnp.where(lane < W_ROW, spread, base_ref[...])


def own_term(omega_ref, u_ref):
    table = [omega_ref[n].astype(F32) for n in range(PARAMS)]
    for m in range(PARAMS):
        total = jnp.zeros(table[0].shape, F32)
        for n in range(PARAMS):
            total = total + u_ref[m, n : n + 1, :] * table[n]
        yield total


def sketch_kernel(solved_ref, omega_ref, u_ref, sketch_ref, gram_ref):
    own = list(own_term(omega_ref, u_ref))
    turned = solved_ref[...].astype(F32).T
    wanted = lax.broadcasted_iota(jnp.int32, turned.shape, 0).astype(F32)
    chosen = jnp.where(wanted == turned[ID_ROW : ID_ROW + 1, :], 1.0, 0.0).astype(BF16)
    tops, rests = [], []
    for m in range(PARAMS):
        part = jnp.zeros((COLS, turned.shape[1]), F32)
        for i in range(3):
            w_row = W_ROW + 3 * m + i
            part = part + turned[w_row : w_row + 1, :] * turned[COLS * i : COLS * (i + 1), :]
        top = part.astype(BF16)
        tops.append(top)
        rests.append((part - top.astype(F32)).astype(BF16))
    summed = dot_lanes(jnp.concatenate(tops + rests, axis=0), chosen)
    half = PARAMS * COLS
    parts = []
    for m in range(PARAMS):
        at = COLS * m
        parts.append(own[m] - (summed[at : at + COLS, :] + summed[half + at : half + at + COLS, :]))
        sketch_ref[m] = parts[m]
    wide = jnp.concatenate(parts, axis=1)
    gram = lax.dot_general(
        wide, wide, (((1,), (1,)), ((), ())), precision=HIGH, preferred_element_type=F32
    )
    packed = jnp.concatenate([gram[8 * q : 8 * q + 8, :] for q in range(4)], axis=1)
    gram_ref[...] = jnp.broadcast_to(packed[None], gram_ref.shape)


def gather_kernel(parts_ref, out_ref):
    out_ref[...] = jnp.broadcast_to(jnp.sum(parts_ref[...], axis=0)[None], out_ref.shape)


def finish_kernel(row_total, parts_ref, sketch_ref, basis_ref, factor_ref):
    packed = jnp.sum(parts_ref[...], axis=0) / row_total
    gram = jnp.concatenate([packed[:, COLS * q : COLS * (q + 1)] for q in range(4)], axis=0)
    row = lax.broadcasted_iota(jnp.int32, (COLS, COLS), 0)
    column = lax.broadcasted_iota(jnp.int32, (COLS, COLS), 1)
    work = jnp.concatenate([gram, jnp.where(row == column, 1.0, 0.0)], axis=1)
    wide_row = lax.broadcasted_iota(jnp.int32, work.shape, 0)
    pivots = jnp.broadcast_to(work[:, 0:1], work.shape)
    for k in range(COLS - 1):
        ahead = jnp.broadcast_to(work[:, k + 1 : k + 2], work.shape)
        below = jnp.where(wide_row > k, pivots, 0.0) * (1.0 / pivots[k : k + 1, :])
        pivots = ahead - below * pivots[k + 1 : k + 2, :]
        work = work - below * work[k : k + 1, :]
    diagonal = jnp.sum(jnp.where(row == column, work[:, :COLS], 0.0), axis=1, keepdims=True)
    work = work * (1.0 / jnp.sqrt(diagonal))
    factor_ref[...] = jnp.where(column >= row, work[:, :COLS], 0.0)
    wide = jnp.concatenate([sketch_ref[m] for m in range(PARAMS)], axis=1)
    basis = jnp.dot(work[:, COLS:], wide, precision=HIGH, preferred_element_type=F32)
    for m in range(PARAMS):
        basis_ref[m] = basis[:, LANES * m : LANES * (m + 1)]


def middle(axes):
    index = 0
    for axis in axes:
        size = lax.axis_size(axis)
        index = index * size + (size // 2 if size > 2 else 0)
    return index


def exchange(values, axes, first=0):
    peers = lax.axis_size(axes)
    parts = values.reshape(peers, values.shape[0] // peers, *values.shape[1:])
    order = list(range(peers))
    order[0], order[first] = first, 0
    parts = lax.all_to_all(
        parts,
        axes,
        split_axis=0,
        concat_axis=0,
        tiled=True,
        axis_index_groups=[order] if first else None,
    )
    return parts.reshape(values.shape)


def on_device(omega, u_blocks, w_blocks, v_inverse, obs_camera, obs_track, obs_mask):
    track_count = lax.axis_size(TRACK)
    cam_count = lax.axis_size(CAM)
    devices = track_count * cam_count
    columns, params, cam_width = omega.shape
    obs = obs_camera.shape[0]
    capacity = max(2, 2 * obs // devices)
    slots = devices * capacity
    tracks = obs // BLK_OBS * TRK_BLK
    by_slot_shape = ((slots, LANES), BF16)

    table = omega.transpose(1, 0, 2)
    tables = lax.all_gather(table.reshape(params * columns, cam_width), CAM)

    head = middle(TRACK)
    block = cam_count * capacity
    request, slot, values = call(
        functools.partial(request_kernel, (capacity, head * block, block)),
        (by_slot_shape, ((1, obs), jnp.int32), ((LANES, obs), BF16)),
        *(
            pltpu.with_memory_space_constraint(x, pltpu.HBM)
            for x in (obs_camera.reshape(1, obs), obs_mask.reshape(1, obs), w_blocks)
        ),
        scratch=(
            pltpu.VMEM((1, obs), jnp.int32),
            pltpu.VMEM((1, obs), jnp.int32),
            pltpu.VMEM(w_blocks.shape, BF16),
            pltpu.VMEM((LANES, obs), F32),
            pltpu.SemaphoreType.DMA((3,)),
        ),
        in_specs=[pl.BlockSpec(memory_space=pltpu.HBM)] * 3,
    )
    asked = exchange(request, TRACK, head)
    (reply,) = call(
        functools.partial(project_kernel, (capacity, head * block, block)),
        (by_slot_shape,),
        asked,
        tables,
        scratch=(pltpu.VMEM((slots, LANES), F32), pltpu.VMEM((slots, LANES), F32)),
    )
    projected = exchange(reply, TRACK)

    by_track, by_slot, base = call(
        member_kernel,
        (((tracks, slots), BF16), ((slots, tracks), BF16), by_slot_shape),
        slot,
        obs_track.reshape(1, obs),
        values,
    )
    (outgoing,) = call(
        solve_kernel, (by_slot_shape,), projected, by_track, by_slot, v_inverse, base
    )
    solved = exchange(outgoing, TRACK_CAM)

    sketch_shape = ((params, columns, cam_width), F32)
    sketch, gram = call(
        sketch_kernel,
        (sketch_shape, ((lax.axis_size(FIRST), 8, LANES), F32)),
        solved,
        table,
        u_blocks,
    )
    gram = exchange(gram, FIRST, middle(FIRST))
    (gram,) = call(gather_kernel, (((lax.axis_size(SECOND), 8, LANES), F32),), gram)
    gram = exchange(gram, SECOND, middle(SECOND))
    basis, factor = call(
        functools.partial(finish_kernel, float(params * cam_width * devices)),
        (sketch_shape, ((columns, columns), F32)),
        gram,
        sketch,
    )
    return (sketch.transpose(1, 0, 2), basis.transpose(1, 0, 2), factor)


def solution(mesh):
    track, cam = mesh.devices.shape
    split = Mesh(
        mesh.devices.reshape(8, track // 8, cam // 2, 2), ("track_0", "track_1", "cam_0", "cam_1")
    )
    return jax.shard_map(
        on_device,
        mesh=split,
        in_specs=(
            P(None, None, TRACK_CAM),
            P(None, None, TRACK_CAM),
            P(None, None, TRACK_CAM),
            P(None, None, TRACK_CAM),
            P(TRACK_CAM),
            P(TRACK_CAM),
            P(TRACK_CAM),
        ),
        out_specs=(P(None, None, TRACK_CAM), P(None, None, TRACK_CAM), P()),
        check_vma=False,
    )
```

```python
import functools

import jax
import jax.numpy as jnp
from jax import lax
from jax.experimental import pallas as pl
from jax.experimental.pallas import tpu as pltpu
from jax.sharding import Mesh
from jax.sharding import PartitionSpec as P

BLK_OBS = 128
TRK_BLK = 32
LANES = 128
PARAMS = 9
COLS = 32
TRACK = ("track_0", "track_1")
CAM = ("cam_0", "cam_1")
TRACK_CAM = TRACK + CAM
FIRST = ("track_1", "cam_1")
SECOND = ("track_0", "cam_0")
W_ROW = 3 * COLS
ID_ROW = W_ROW + 3 * PARAMS
HIGH = lax.Precision.HIGHEST
F32 = jnp.float32
BF16 = jnp.bfloat16


def dot_lanes(lhs, rhs):
    return lax.dot_general(lhs, rhs, (((1,), (1,)), ((), ())), preferred_element_type=F32)


def call(kernel, shapes, *args, scratch=(), in_specs=None):
    specs = {} if in_specs is None else {"in_specs": in_specs}
    return pl.pallas_call(
        kernel,
        out_shape=tuple(jax.ShapeDtypeStruct(s, d) for s, d in shapes),
        scratch_shapes=list(scratch),
        compiler_params=pltpu.CompilerParams(vmem_limit_bytes=32 << 20),
        **specs,
    )(*args)


def request_kernel(
    sizes,
    camera_hbm,
    mask_hbm,
    w_hbm,
    track_hbm,
    request_ref,
    slot_ref,
    values_ref,
    camera_ref,
    mask_ref,
    w_ref,
    track_ref,
    rows,
    sems,
):
    capacity, head, block = sizes
    copies = [
        pltpu.make_async_copy(source, target, sems.at[n])
        for n, (source, target) in enumerate(
            ((camera_hbm, camera_ref), (mask_hbm, mask_ref), (w_hbm, w_ref), (track_hbm, track_ref))
        )
    ]
    for copy in copies:
        copy.start()
    rows[...] = jnp.zeros(rows.shape, F32)
    for copy in copies:
        copy.wait()
    obs = camera_ref.shape[1]
    camera = camera_ref[...]
    owner = lax.shift_right_logical(camera, 7)
    owner_f = owner.astype(F32)
    blocks = obs // LANES
    sub = lax.broadcasted_iota(jnp.int32, (LANES, LANES), 0)
    lane = lax.broadcasted_iota(jnp.int32, (LANES, LANES), 1)
    row_of = [owner_f[:, LANES * b : LANES * (b + 1)] for b in range(blocks)]
    column_of = [jnp.broadcast_to(r, (LANES, LANES)).T for r in row_of]
    ranks = []
    for q in range(blocks):
        same = jnp.where((column_of[q] == row_of[q]) & (sub < lane), 1.0, 0.0)
        for b in range(q):
            same = same + jnp.where(column_of[b] == row_of[q], 1.0, 0.0)
        ranks.append(jnp.sum(same, axis=0, keepdims=True))
    slot = owner * capacity + jnp.concatenate(ranks, axis=1).astype(jnp.int32)
    slot_ref[0:1, :] = slot
    slot_ref[1:2, :] = track_ref[...]
    at_head = (slot >= head) & (slot < head + block)
    slot = jnp.where(slot < block, slot + head, jnp.where(at_head, slot - head, slot))
    live = mask_ref[...].astype(F32)
    for m in range(PARAMS):
        rows[W_ROW + 3 * m : W_ROW + 3 * m + 3, :] = w_ref[m].astype(F32) * live
    rows[ID_ROW : ID_ROW + 1, :] = (camera & (LANES - 1)).astype(F32)
    values = rows[...].astype(BF16)
    values_ref[...] = values
    slots = request_ref.shape[0]
    step = 256
    for s in range(0, slots, step):
        ids = lax.broadcasted_iota(jnp.int32, (step, obs), 0) + s
        chosen = jnp.where(ids == slot, 1.0, 0.0).astype(BF16)
        request_ref[s : s + step, :] = dot_lanes(chosen, values).astype(BF16)


def member_kernel(slot_ref, values_ref, by_track_ref, by_slot_ref, base_ref):
    obs = slot_ref.shape[1]
    tracks, slots = by_track_ref.shape
    position = lax.broadcasted_iota(jnp.int32, (1, obs), 1)
    track = lax.shift_right_logical(position, 7) * TRK_BLK + slot_ref[1:2, :]
    ids = lax.broadcasted_iota(jnp.int32, (tracks, obs), 0)
    member = jnp.where(ids == track, 1.0, 0.0).astype(BF16)
    step = 256
    for s in range(0, slots, step):
        ids = lax.broadcasted_iota(jnp.int32, (step, obs), 0) + s
        chosen = jnp.where(ids == slot_ref[0:1, :], 1.0, 0.0).astype(BF16)
        by_track_ref[:, s : s + step] = dot_lanes(member, chosen).astype(BF16)
        by_slot_ref[s : s + step, :] = dot_lanes(chosen, member).astype(BF16)
        base_ref[s : s + step, :] = dot_lanes(chosen, values_ref[...]).astype(BF16)


def dot(lhs, rhs):
    return jnp.dot(lhs, rhs, preferred_element_type=F32)


def project_kernel(sizes, request_ref, table_ref, reply_ref, rows, out_rows):
    capacity, head, block = sizes
    cams = table_ref.shape[0]
    slots = request_ref.shape[0]
    tracks = slots // (cams * capacity)
    rows[...] = request_ref[...].astype(F32)
    for b in range(cams):
        places = [pl.ds(b * capacity + r, tracks, stride=cams * capacity) for r in range(capacity)]
        turned = jnp.concatenate([rows[p, :] for p in places], axis=0).T
        wanted = lax.broadcasted_iota(jnp.int32, turned.shape, 0).astype(F32)
        chosen = jnp.where(wanted == turned[ID_ROW : ID_ROW + 1, :], 1.0, 0.0).astype(BF16)
        found = dot(table_ref[b], chosen)
        parts = []
        for i in range(3):
            part = jnp.zeros((COLS, turned.shape[1]), F32)
            for m in range(PARAMS):
                w_row = W_ROW + 3 * m + i
                part = part + turned[w_row : w_row + 1, :] * found[COLS * m : COLS * (m + 1), :]
            parts.append(part)
        parts.append(jnp.zeros((LANES - 3 * COLS, turned.shape[1]), F32))
        projected = jnp.concatenate(parts, axis=0).T
        for r, place in enumerate(places):
            out_rows[place, :] = projected[r * tracks : (r + 1) * tracks, :]
    reply_ref[...] = out_rows[...].astype(BF16)
    reply_ref[0:block, :] = out_rows[head : head + block, :].astype(BF16)
    reply_ref[head : head + block, :] = out_rows[0:block, :].astype(BF16)


def solve_kernel(
    reply_ref, slot_ref, values_ref, v_ref, out_ref, by_track_ref, by_slot_ref, base_ref
):
    member_kernel(slot_ref, values_ref, by_track_ref, by_slot_ref, base_ref)
    summed = dot(by_track_ref[...], reply_ref[...]).T
    parts = []
    for i in range(3):
        part = jnp.zeros((COLS, LANES), F32)
        for k in range(3):
            part = part + v_ref[i, k : k + 1, :] * summed[COLS * k : COLS * (k + 1), :]
        parts.append(part)
    parts.append(jnp.zeros((LANES - 3 * COLS, LANES), F32))
    solved = jnp.concatenate(parts, axis=0).astype(BF16)
    spread = dot_lanes(by_slot_ref[...], solved).astype(BF16)
    lane = lax.broadcasted_iota(jnp.int32, spread.shape, 1)
    out_ref[...] = jnp.where(lane < W_ROW, spread, base_ref[...])


def own_term(omega_ref, u_ref):
    table = [omega_ref[n].astype(F32) for n in range(PARAMS)]
    for m in range(PARAMS):
        total = jnp.zeros(table[0].shape, F32)
        for n in range(PARAMS):
            total = total + u_ref[m, n : n + 1, :] * table[n]
        yield total


def sketch_kernel(solved_ref, omega_ref, u_ref, sketch_ref, gram_ref):
    own = list(own_term(omega_ref, u_ref))
    turned = solved_ref[...].astype(F32).T
    wanted = lax.broadcasted_iota(jnp.int32, turned.shape, 0).astype(F32)
    chosen = jnp.where(wanted == turned[ID_ROW : ID_ROW + 1, :], 1.0, 0.0).astype(BF16)
    tops, rests = [], []
    for m in range(PARAMS):
        part = jnp.zeros((COLS, turned.shape[1]), F32)
        for i in range(3):
            w_row = W_ROW + 3 * m + i
            part = part + turned[w_row : w_row + 1, :] * turned[COLS * i : COLS * (i + 1), :]
        top = part.astype(BF16)
        tops.append(top)
        rests.append((part - top.astype(F32)).astype(BF16))
    summed = dot_lanes(jnp.concatenate(tops + rests, axis=0), chosen)
    half = PARAMS * COLS
    parts = []
    for m in range(PARAMS):
        at = COLS * m
        parts.append(own[m] - (summed[at : at + COLS, :] + summed[half + at : half + at + COLS, :]))
        sketch_ref[m] = parts[m]
    wide = jnp.concatenate(parts, axis=1)
    gram = lax.dot_general(
        wide, wide, (((1,), (1,)), ((), ())), precision=HIGH, preferred_element_type=F32
    )
    packed = jnp.concatenate([gram[8 * q : 8 * q + 8, :] for q in range(4)], axis=1)
    gram_ref[...] = jnp.broadcast_to(packed[None], gram_ref.shape)


def gather_kernel(parts_ref, out_ref):
    out_ref[...] = jnp.broadcast_to(jnp.sum(parts_ref[...], axis=0)[None], out_ref.shape)


def finish_kernel(row_total, parts_ref, sketch_ref, basis_ref, factor_ref):
    packed = jnp.sum(parts_ref[...], axis=0) / row_total
    gram = jnp.concatenate([packed[:, COLS * q : COLS * (q + 1)] for q in range(4)], axis=0)
    row = lax.broadcasted_iota(jnp.int32, (COLS, COLS), 0)
    column = lax.broadcasted_iota(jnp.int32, (COLS, COLS), 1)
    work = jnp.concatenate([gram, jnp.where(row == column, 1.0, 0.0)], axis=1)
    wide_row = lax.broadcasted_iota(jnp.int32, work.shape, 0)
    pivots = jnp.broadcast_to(work[:, 0:1], work.shape)
    for k in range(COLS - 1):
        ahead = jnp.broadcast_to(work[:, k + 1 : k + 2], work.shape)
        below = jnp.where(wide_row > k, pivots, 0.0) * (1.0 / pivots[k : k + 1, :])
        pivots = ahead - below * pivots[k + 1 : k + 2, :]
        work = work - below * work[k : k + 1, :]
    diagonal = jnp.sum(jnp.where(row == column, work[:, :COLS], 0.0), axis=1, keepdims=True)
    work = work * (1.0 / jnp.sqrt(diagonal))
    factor_ref[...] = jnp.where(column >= row, work[:, :COLS], 0.0)
    wide = jnp.concatenate([sketch_ref[m] for m in range(PARAMS)], axis=1)
    basis = jnp.dot(work[:, COLS:], wide, precision=HIGH, preferred_element_type=F32)
    for m in range(PARAMS):
        basis_ref[m] = basis[:, LANES * m : LANES * (m + 1)]


def middle(axes):
    index = 0
    for axis in axes:
        size = lax.axis_size(axis)
        index = index * size + (size // 2 if size > 2 else 0)
    return index


def exchange(values, axes, first=0):
    peers = lax.axis_size(axes)
    parts = values.reshape(peers, values.shape[0] // peers, *values.shape[1:])
    order = list(range(peers))
    order[0], order[first] = first, 0
    parts = lax.all_to_all(
        parts,
        axes,
        split_axis=0,
        concat_axis=0,
        tiled=True,
        axis_index_groups=[order] if first else None,
    )
    return parts.reshape(values.shape)


def on_device(omega, u_blocks, w_blocks, v_inverse, obs_camera, obs_track, obs_mask):
    track_count = lax.axis_size(TRACK)
    cam_count = lax.axis_size(CAM)
    devices = track_count * cam_count
    columns, params, cam_width = omega.shape
    obs = obs_camera.shape[0]
    capacity = max(2, 2 * obs // devices)
    slots = devices * capacity
    tracks = obs // BLK_OBS * TRK_BLK
    by_slot_shape = ((slots, LANES), BF16)

    table = omega.transpose(1, 0, 2)
    tables = lax.all_gather(table.reshape(params * columns, cam_width), CAM)

    head = middle(TRACK)
    block = cam_count * capacity
    request, slot, values = call(
        functools.partial(request_kernel, (capacity, head * block, block)),
        (by_slot_shape, ((2, obs), jnp.int32), ((LANES, obs), BF16)),
        *(
            pltpu.with_memory_space_constraint(x, pltpu.HBM)
            for x in (
                obs_camera.reshape(1, obs),
                obs_mask.reshape(1, obs),
                w_blocks,
                obs_track.reshape(1, obs),
            )
        ),
        scratch=(
            pltpu.VMEM((1, obs), jnp.int32),
            pltpu.VMEM((1, obs), jnp.int32),
            pltpu.VMEM(w_blocks.shape, BF16),
            pltpu.VMEM((1, obs), jnp.int32),
            pltpu.VMEM((LANES, obs), F32),
            pltpu.SemaphoreType.DMA((4,)),
        ),
        in_specs=[pl.BlockSpec(memory_space=pltpu.HBM)] * 4,
    )
    asked = exchange(request, TRACK, head)
    (reply,) = call(
        functools.partial(project_kernel, (capacity, head * block, block)),
        (by_slot_shape,),
        asked,
        tables,
        scratch=(pltpu.VMEM((slots, LANES), F32), pltpu.VMEM((slots, LANES), F32)),
    )
    projected = exchange(reply, TRACK)

    (outgoing,) = call(
        solve_kernel,
        (by_slot_shape,),
        projected,
        slot,
        values,
        v_inverse,
        scratch=(
            pltpu.VMEM((tracks, slots), BF16),
            pltpu.VMEM((slots, tracks), BF16),
            pltpu.VMEM((slots, LANES), BF16),
        ),
    )
    solved = exchange(outgoing, TRACK_CAM)

    sketch_shape = ((params, columns, cam_width), F32)
    sketch, gram = call(
        sketch_kernel,
        (sketch_shape, ((lax.axis_size(FIRST), 8, LANES), F32)),
        solved,
        table,
        u_blocks,
    )
    gram = exchange(gram, FIRST, middle(FIRST))
    (gram,) = call(gather_kernel, (((lax.axis_size(SECOND), 8, LANES), F32),), gram)
    gram = exchange(gram, SECOND, middle(SECOND))
    basis, factor = call(
        functools.partial(finish_kernel, float(params * cam_width * devices)),
        (sketch_shape, ((columns, columns), F32)),
        gram,
        sketch,
    )
    return (sketch.transpose(1, 0, 2), basis.transpose(1, 0, 2), factor)


def solution(mesh):
    track, cam = mesh.devices.shape
    split = Mesh(
        mesh.devices.reshape(8, track // 8, cam // 2, 2), ("track_0", "track_1", "cam_0", "cam_1")
    )
    return jax.shard_map(
        on_device,
        mesh=split,
        in_specs=(
            P(None, None, TRACK_CAM),
            P(None, None, TRACK_CAM),
            P(None, None, TRACK_CAM),
            P(None, None, TRACK_CAM),
            P(TRACK_CAM),
            P(TRACK_CAM),
            P(TRACK_CAM),
        ),
        out_specs=(P(None, None, TRACK_CAM), P(None, None, TRACK_CAM), P()),
        check_vma=False,
    )
```

```python
import functools

import jax
import jax.numpy as jnp
from jax import lax
from jax.experimental import pallas as pl
from jax.experimental.pallas import tpu as pltpu
from jax.sharding import Mesh
from jax.sharding import PartitionSpec as P

BLK_OBS = 128
TRK_BLK = 32
LANES = 128
PARAMS = 9
COLS = 32
TRACK = ("track_0", "track_1")
CAM = ("cam_0", "cam_1")
TRACK_CAM = TRACK + CAM
FIRST = ("track_1", "cam_1")
SECOND = ("track_0", "cam_0")
W_ROW = 3 * COLS
ID_ROW = W_ROW + 3 * PARAMS
HIGH = lax.Precision.HIGHEST
F32 = jnp.float32
BF16 = jnp.bfloat16


def dot_lanes(lhs, rhs):
    return lax.dot_general(lhs, rhs, (((1,), (1,)), ((), ())), preferred_element_type=F32)


def call(kernel, shapes, *args, scratch=(), in_specs=None):
    specs = {} if in_specs is None else {"in_specs": in_specs}
    return pl.pallas_call(
        kernel,
        out_shape=tuple(jax.ShapeDtypeStruct(s, d) for s, d in shapes),
        scratch_shapes=list(scratch),
        compiler_params=pltpu.CompilerParams(vmem_limit_bytes=32 << 20),
        **specs,
    )(*args)


def request_kernel(
    sizes,
    camera_hbm,
    mask_hbm,
    w_hbm,
    track_hbm,
    request_ref,
    slot_ref,
    values_ref,
    camera_ref,
    mask_ref,
    w_ref,
    track_ref,
    rows,
    sems,
):
    capacity, head, block = sizes
    copies = [
        pltpu.make_async_copy(source, target, sems.at[n])
        for n, (source, target) in enumerate(
            ((camera_hbm, camera_ref), (mask_hbm, mask_ref), (w_hbm, w_ref), (track_hbm, track_ref))
        )
    ]
    for copy in copies:
        copy.start()
    rows[...] = jnp.zeros(rows.shape, F32)
    for copy in copies:
        copy.wait()
    obs = camera_ref.shape[1]
    camera = camera_ref[...]
    owner = lax.shift_right_logical(camera, 7)
    owner_f = owner.astype(F32)
    blocks = obs // LANES
    sub = lax.broadcasted_iota(jnp.int32, (LANES, LANES), 0)
    lane = lax.broadcasted_iota(jnp.int32, (LANES, LANES), 1)
    row_of = [owner_f[:, LANES * b : LANES * (b + 1)] for b in range(blocks)]
    column_of = [jnp.broadcast_to(r, (LANES, LANES)).T for r in row_of]
    ranks = []
    for q in range(blocks):
        same = jnp.where((column_of[q] == row_of[q]) & (sub < lane), 1.0, 0.0)
        for b in range(q):
            same = same + jnp.where(column_of[b] == row_of[q], 1.0, 0.0)
        ranks.append(jnp.sum(same, axis=0, keepdims=True))
    slot = owner * capacity + jnp.concatenate(ranks, axis=1).astype(jnp.int32)
    slot_ref[0:1, :] = slot
    slot_ref[1:2, :] = track_ref[...]
    at_head = (slot >= head) & (slot < head + block)
    slot = jnp.where(slot < block, slot + head, jnp.where(at_head, slot - head, slot))
    live = mask_ref[...].astype(F32)
    for m in range(PARAMS):
        rows[W_ROW + 3 * m : W_ROW + 3 * m + 3, :] = w_ref[m].astype(F32) * live
    rows[ID_ROW : ID_ROW + 1, :] = (camera & (LANES - 1)).astype(F32)
    values = rows[...].astype(BF16)
    values_ref[...] = values
    slots = request_ref.shape[0]
    step = 256
    for s in range(0, slots, step):
        ids = lax.broadcasted_iota(jnp.int32, (step, obs), 0) + s
        chosen = jnp.where(ids == slot, 1.0, 0.0).astype(BF16)
        request_ref[s : s + step, :] = dot_lanes(chosen, values).astype(BF16)


def member_kernel(slot_ref, values_ref, by_track_ref, by_slot_ref, base_ref):
    obs = slot_ref.shape[1]
    tracks, slots = by_track_ref.shape
    position = lax.broadcasted_iota(jnp.int32, (1, obs), 1)
    track = lax.shift_right_logical(position, 7) * TRK_BLK + slot_ref[1:2, :]
    ids = lax.broadcasted_iota(jnp.int32, (tracks, obs), 0)
    member = jnp.where(ids == track, 1.0, 0.0).astype(BF16)
    step = 256
    for s in range(0, slots, step):
        ids = lax.broadcasted_iota(jnp.int32, (step, obs), 0) + s
        chosen = jnp.where(ids == slot_ref[0:1, :], 1.0, 0.0).astype(BF16)
        by_track_ref[:, s : s + step] = dot_lanes(member, chosen).astype(BF16)
        by_slot_ref[s : s + step, :] = dot_lanes(chosen, member).astype(BF16)
        base_ref[s : s + step, :] = dot_lanes(chosen, values_ref[...]).astype(BF16)


def dot(lhs, rhs):
    return jnp.dot(lhs, rhs, preferred_element_type=F32)


def three_parts(values):
    top = values.astype(BF16)
    rest = values - top.astype(F32)
    second = rest.astype(BF16)
    return [top, second, (rest - second.astype(F32)).astype(BF16)]


def project_kernel(sizes, request_ref, table_ref, reply_ref, rows, out_rows):
    capacity, head, block = sizes
    cams = table_ref.shape[0]
    slots = request_ref.shape[0]
    tracks = slots // (cams * capacity)
    rows[...] = request_ref[...].astype(F32)
    for b in range(cams):
        places = [pl.ds(b * capacity + r, tracks, stride=cams * capacity) for r in range(capacity)]
        turned = jnp.concatenate([rows[p, :] for p in places], axis=0).T
        wanted = lax.broadcasted_iota(jnp.int32, turned.shape, 0).astype(F32)
        chosen = jnp.where(wanted == turned[ID_ROW : ID_ROW + 1, :], 1.0, 0.0).astype(BF16)
        found = dot(table_ref[b], chosen)
        parts = []
        for i in range(3):
            part = jnp.zeros((COLS, turned.shape[1]), F32)
            for m in range(PARAMS):
                w_row = W_ROW + 3 * m + i
                part = part + turned[w_row : w_row + 1, :] * found[COLS * m : COLS * (m + 1), :]
            parts.append(part)
        parts.append(jnp.zeros((LANES - 3 * COLS, turned.shape[1]), F32))
        projected = jnp.concatenate(parts, axis=0).T
        for r, place in enumerate(places):
            out_rows[place, :] = projected[r * tracks : (r + 1) * tracks, :]
    reply_ref[...] = out_rows[...].astype(BF16)
    reply_ref[0:block, :] = out_rows[head : head + block, :].astype(BF16)
    reply_ref[head : head + block, :] = out_rows[0:block, :].astype(BF16)


def solve_kernel(
    reply_ref, slot_ref, values_ref, v_ref, out_ref, by_track_ref, by_slot_ref, base_ref
):
    member_kernel(slot_ref, values_ref, by_track_ref, by_slot_ref, base_ref)
    summed = dot(by_track_ref[...], reply_ref[...]).T
    parts = []
    for i in range(3):
        part = jnp.zeros((COLS, LANES), F32)
        for k in range(3):
            part = part + v_ref[i, k : k + 1, :] * summed[COLS * k : COLS * (k + 1), :]
        parts.append(part)
    parts.append(jnp.zeros((LANES - 3 * COLS, LANES), F32))
    solved = jnp.concatenate(parts, axis=0).astype(BF16)
    spread = dot_lanes(by_slot_ref[...], solved).astype(BF16)
    lane = lax.broadcasted_iota(jnp.int32, spread.shape, 1)
    out_ref[...] = jnp.where(lane < W_ROW, spread, base_ref[...])


def own_term(omega_ref, u_ref):
    table = [omega_ref[n].astype(F32) for n in range(PARAMS)]
    for m in range(PARAMS):
        total = jnp.zeros(table[0].shape, F32)
        for n in range(PARAMS):
            total = total + u_ref[m, n : n + 1, :] * table[n]
        yield total


def sketch_kernel(solved_ref, omega_ref, u_ref, sketch_ref, gram_ref):
    own = list(own_term(omega_ref, u_ref))
    turned = solved_ref[...].astype(F32).T
    wanted = lax.broadcasted_iota(jnp.int32, turned.shape, 0).astype(F32)
    chosen = jnp.where(wanted == turned[ID_ROW : ID_ROW + 1, :], 1.0, 0.0).astype(BF16)
    tops, rests = [], []
    for m in range(PARAMS):
        part = jnp.zeros((COLS, turned.shape[1]), F32)
        for i in range(3):
            w_row = W_ROW + 3 * m + i
            part = part + turned[w_row : w_row + 1, :] * turned[COLS * i : COLS * (i + 1), :]
        top = part.astype(BF16)
        tops.append(top)
        rests.append((part - top.astype(F32)).astype(BF16))
    summed = dot_lanes(jnp.concatenate(tops + rests, axis=0), chosen)
    half = PARAMS * COLS
    parts = []
    for m in range(PARAMS):
        at = COLS * m
        parts.append(own[m] - (summed[at : at + COLS, :] + summed[half + at : half + at + COLS, :]))
        sketch_ref[m] = parts[m]
    wide = jnp.concatenate(parts, axis=1)
    stacked = jnp.concatenate(three_parts(wide), axis=0)
    products = dot_lanes(stacked, stacked)
    gram = jnp.zeros((COLS, COLS), F32)
    for p, q in ((2, 2), (1, 2), (2, 1), (0, 2), (1, 1), (2, 0), (0, 1), (1, 0), (0, 0)):
        gram = gram + products[COLS * p : COLS * (p + 1), COLS * q : COLS * (q + 1)]
    packed = jnp.concatenate([gram[8 * q : 8 * q + 8, :] for q in range(4)], axis=1)
    gram_ref[...] = jnp.broadcast_to(packed[None], gram_ref.shape)


def gather_kernel(parts_ref, out_ref):
    out_ref[...] = jnp.broadcast_to(jnp.sum(parts_ref[...], axis=0)[None], out_ref.shape)


def finish_kernel(row_total, parts_ref, sketch_ref, basis_ref, factor_ref):
    packed = jnp.sum(parts_ref[...], axis=0) / row_total
    gram = jnp.concatenate([packed[:, COLS * q : COLS * (q + 1)] for q in range(4)], axis=0)
    row = lax.broadcasted_iota(jnp.int32, (COLS, COLS), 0)
    column = lax.broadcasted_iota(jnp.int32, (COLS, COLS), 1)
    work = jnp.concatenate([gram, jnp.where(row == column, 1.0, 0.0)], axis=1)
    wide_row = lax.broadcasted_iota(jnp.int32, work.shape, 0)
    pivots = jnp.broadcast_to(work[:, 0:1], work.shape)
    for k in range(COLS - 1):
        ahead = jnp.broadcast_to(work[:, k + 1 : k + 2], work.shape)
        below = jnp.where(wide_row > k, pivots, 0.0) * (1.0 / pivots[k : k + 1, :])
        pivots = ahead - below * pivots[k + 1 : k + 2, :]
        work = work - below * work[k : k + 1, :]
    diagonal = jnp.sum(jnp.where(row == column, work[:, :COLS], 0.0), axis=1, keepdims=True)
    work = work * (1.0 / jnp.sqrt(diagonal))
    factor_ref[...] = jnp.where(column >= row, work[:, :COLS], 0.0)
    wide = jnp.concatenate([sketch_ref[m] for m in range(PARAMS)], axis=1)
    basis = jnp.dot(work[:, COLS:], wide, precision=HIGH, preferred_element_type=F32)
    for m in range(PARAMS):
        basis_ref[m] = basis[:, LANES * m : LANES * (m + 1)]


def middle(axes):
    index = 0
    for axis in axes:
        size = lax.axis_size(axis)
        index = index * size + (size // 2 if size > 2 else 0)
    return index


def exchange(values, axes, first=0):
    peers = lax.axis_size(axes)
    parts = values.reshape(peers, values.shape[0] // peers, *values.shape[1:])
    order = list(range(peers))
    order[0], order[first] = first, 0
    parts = lax.all_to_all(
        parts,
        axes,
        split_axis=0,
        concat_axis=0,
        tiled=True,
        axis_index_groups=[order] if first else None,
    )
    return parts.reshape(values.shape)


def on_device(omega, u_blocks, w_blocks, v_inverse, obs_camera, obs_track, obs_mask):
    track_count = lax.axis_size(TRACK)
    cam_count = lax.axis_size(CAM)
    devices = track_count * cam_count
    columns, params, cam_width = omega.shape
    obs = obs_camera.shape[0]
    capacity = max(2, 2 * obs // devices)
    slots = devices * capacity
    tracks = obs // BLK_OBS * TRK_BLK
    by_slot_shape = ((slots, LANES), BF16)

    table = omega.transpose(1, 0, 2)
    tables = lax.all_gather(table.reshape(params * columns, cam_width), CAM)

    head = middle(TRACK)
    block = cam_count * capacity
    request, slot, values = call(
        functools.partial(request_kernel, (capacity, head * block, block)),
        (by_slot_shape, ((2, obs), jnp.int32), ((LANES, obs), BF16)),
        *(
            pltpu.with_memory_space_constraint(x, pltpu.HBM)
            for x in (
                obs_camera.reshape(1, obs),
                obs_mask.reshape(1, obs),
                w_blocks,
                obs_track.reshape(1, obs),
            )
        ),
        scratch=(
            pltpu.VMEM((1, obs), jnp.int32),
            pltpu.VMEM((1, obs), jnp.int32),
            pltpu.VMEM(w_blocks.shape, BF16),
            pltpu.VMEM((1, obs), jnp.int32),
            pltpu.VMEM((LANES, obs), F32),
            pltpu.SemaphoreType.DMA((4,)),
        ),
        in_specs=[pl.BlockSpec(memory_space=pltpu.HBM)] * 4,
    )
    asked = exchange(request, TRACK, head)
    (reply,) = call(
        functools.partial(project_kernel, (capacity, head * block, block)),
        (by_slot_shape,),
        asked,
        tables,
        scratch=(pltpu.VMEM((slots, LANES), F32), pltpu.VMEM((slots, LANES), F32)),
    )
    projected = exchange(reply, TRACK)

    (outgoing,) = call(
        solve_kernel,
        (by_slot_shape,),
        projected,
        slot,
        values,
        v_inverse,
        scratch=(
            pltpu.VMEM((tracks, slots), BF16),
            pltpu.VMEM((slots, tracks), BF16),
            pltpu.VMEM((slots, LANES), BF16),
        ),
    )
    solved = exchange(outgoing, TRACK_CAM)

    sketch_shape = ((params, columns, cam_width), F32)
    sketch, gram = call(
        sketch_kernel,
        (sketch_shape, ((lax.axis_size(FIRST), 8, LANES), F32)),
        solved,
        table,
        u_blocks,
    )
    gram = exchange(gram, FIRST, middle(FIRST))
    (gram,) = call(gather_kernel, (((lax.axis_size(SECOND), 8, LANES), F32),), gram)
    gram = exchange(gram, SECOND, middle(SECOND))
    basis, factor = call(
        functools.partial(finish_kernel, float(params * cam_width * devices)),
        (sketch_shape, ((columns, columns), F32)),
        gram,
        sketch,
    )
    return (sketch.transpose(1, 0, 2), basis.transpose(1, 0, 2), factor)


def solution(mesh):
    track, cam = mesh.devices.shape
    split = Mesh(
        mesh.devices.reshape(8, track // 8, cam // 2, 2), ("track_0", "track_1", "cam_0", "cam_1")
    )
    return jax.shard_map(
        on_device,
        mesh=split,
        in_specs=(
            P(None, None, TRACK_CAM),
            P(None, None, TRACK_CAM),
            P(None, None, TRACK_CAM),
            P(None, None, TRACK_CAM),
            P(TRACK_CAM),
            P(TRACK_CAM),
            P(TRACK_CAM),
        ),
        out_specs=(P(None, None, TRACK_CAM), P(None, None, TRACK_CAM), P()),
        check_vma=False,
    )
```
